128 devices in a mesh: mode: 32 (over z, y, core), slab: 4 (over x).
Axes of the slice: x: 4, y: 4, z: 4, core: 2. Of those that a mesh axis runs over, the one named last changes fastest.
Arguments:
- guess: float32 [4096, 128, 128], P('mode', 'slab'), may hold values from -6 to 6
- right_side: float32 [4096, 128, 128], P('mode', 'slab'), may hold values from -6 to 6
- mean_coef: float32 [128, 128], P('slab'), may hold values from 0.5 to 2
- field_coef: float32 [3, 128, 128], P(None, 'slab'), may hold values from -2.5 to 2.5
- coupling: bfloat16 [32, 16, 128, 128], replicated, may hold values from -0.0625 to 0.0625
- coupling_list: int32 [32, 16], replicated, may hold values from 0 to 95, as said below
- pair_count: int32 [32], replicated, may hold values from 4 to 16, as said below
Outputs:
- solution: float32 [4096, 128, 128], P('mode', 'slab')
- residual: float32 [4096, 128, 128], P('mode', 'slab')
The draws below stay inside these ranges and needn't reach their ends.
Inputs may be any that keep to these rules, and one draw needn't show every extreme that they name: `coupling_list`: each row holds 16 distinct entries; entry e couples its row's mode block to mode block e // 3 through coefficient field e % 3. Only the first pair_count entries of a row are live. `pair_count`: number of live entries of each mode block's row.
All inputs are finite; a program needn't handle non-finite values.
Results may differ from the reference program's by a relative error of at most 0.0012.
Values may be sent and summed in bfloat16 or wider, within the bound.
A program may use at most 256 MiB of HBM per device.

```python
import math
import jax
import jax.numpy as jnp
from jax import lax

BLK = 128
FIELDS = 3
MAXC = 16
NX = 128
NY = 128
ITERS = 2
BLOCKS = 32
MODES = 4096


def move_front(entries, value, slot):
    position = jnp.argmax(entries == value)
    displaced = entries[slot]
    return entries.at[slot].set(value).at[position].set(displaced)


def draw_coupling_list(key, part):
    pair_total = BLOCKS * FIELDS
    row_keys = jax.random.split(jax.random.fold_in(key, 11), BLOCKS)
    shuffled = jax.vmap(lambda single: jax.random.permutation(single, pair_total))(row_keys)
    chosen = jax.random.randint(jax.random.fold_in(key, 12), (), 0, BLOCKS)
    special = move_front(shuffled[chosen], pair_total - 1, 0)
    special = move_front(special, 0, 1)
    shuffled = shuffled.at[chosen].set(special)
    return shuffled[:, :MAXC].astype(jnp.int32)


def draw_pair_count(key, part):
    lowest = MAXC // 4
    counts = jax.random.randint(jax.random.fold_in(key, 21), (BLOCKS,), lowest, MAXC + 1)
    first = jax.random.randint(jax.random.fold_in(key, 22), (), 0, BLOCKS)
    offset = jax.random.randint(jax.random.fold_in(key, 23), (), 1, BLOCKS)
    second = (first + offset) % BLOCKS
    counts = counts.at[first].set(MAXC).at[second].set(lowest)
    return counts.astype(jnp.int32)


def level_of(rng, extent, pieces, low, largest):
    def one(dim, shards_of):
        draws = jax.random.uniform(jax.random.fold_in(jax.random.fold_in(rng, 6), dim), (shards_of,), jnp.float32, low / len(pieces), largest / len(pieces))
        return jnp.repeat(jnp.exp(draws), extent[dim] // shards_of).reshape((-1,) + (1,) * (len(extent) - dim - 1))

    gain = one(*pieces[0])
    for cut in pieces[1:]:
        gain = gain * one(*cut)
    return gain


def normal_values(rng, extent, width, bound, pieces=(), kind=jnp.bfloat16):
    gain = level_of(rng, extent, pieces, -0.22, 0.18) if pieces else 1.0
    values = jax.random.normal(rng, extent, jnp.float32) * width * gain
    return jnp.minimum(jnp.maximum(values, -bound), bound).astype(kind)


def setup_inputs(seed: int = 0) -> dict:
    splits = jax.random.split(jax.random.key(seed), 8)
    guess = normal_values(splits[0], (MODES, NX, NY), 1.0, 6.0, ((0, 32), (1, 4)), jnp.float32)
    right_side = normal_values(splits[1], (MODES, NX, NY), 1.0, 6.0, ((0, 32), (1, 4)), jnp.float32)
    mean_coef = jnp.clip(jnp.exp(math.log(2.0) - 1.3862944 * jax.random.uniform(splits[2], (NX, NY), jnp.float32) ** level_of(splits[2], (NX, NY), ((0, 4),), -0.2, 0.2)), 0.5, 2.0)
    field_coef = normal_values(splits[3], (FIELDS, NX, NY), 0.5, 2.5, ((1, 4),), jnp.float32)
    coupling = normal_values(splits[4], (BLOCKS, MAXC, BLK, BLK), (4 * BLK * MAXC) ** -0.5, 0.0625)
    coupling_list = draw_coupling_list(jax.random.fold_in(splits[7], 71), 0)
    pair_count = draw_pair_count(jax.random.fold_in(splits[7], 71), 0)
    return {"guess": guess, "right_side": right_side, "mean_coef": mean_coef, "field_coef": field_coef, "coupling": coupling, "coupling_list": coupling_list, "pair_count": pair_count}


relaxation = 0.6

def operate(padded, coef_pad):
    center = coef_pad[..., 1:-1, :]
    field = padded[..., 1:-1, :]
    result = 0.5 * (center + coef_pad[..., :-2, :]) * (field - padded[..., :-2, :])
    result = result + 0.5 * (center + coef_pad[..., 2:, :]) * (field - padded[..., 2:, :])
    side_coef = jnp.pad(center, [(0, 0)] * (center.ndim - 1) + [(1, 1)], mode='edge')
    side_field = jnp.pad(field, [(0, 0)] * (field.ndim - 1) + [(1, 1)])
    result = result + 0.5 * (center + side_coef[..., :-2]) * (field - side_field[..., :-2])
    result = result + 0.5 * (center + side_coef[..., 2:]) * (field - side_field[..., 2:])
    return result

def sine_table(length):
    counter = jnp.arange(length).astype(jnp.float32) + 1.0
    angle = math.pi * counter[:, None] * counter[None, :] / (length + 1)
    return math.sqrt(2.0 / (length + 1)) * jnp.sin(angle)

def eigen_table(first, second):
    along_first = 2.0 * jnp.cos(math.pi * (jnp.arange(first).astype(jnp.float32) + 1.0) / (first + 1))
    along_second = 2.0 * jnp.cos(math.pi * (jnp.arange(second).astype(jnp.float32) + 1.0) / (second + 1))
    return 4.0 - along_first[:, None] - along_second[None, :]

def mean_solve(resid):
    highest = lax.Precision.HIGHEST
    rows_table = sine_table(NX)
    cols_table = sine_table(NY)
    spectral = jnp.einsum('px,mxy->mpy', rows_table, resid, precision=highest)
    spectral = jnp.einsum('mpy,yq->mpq', spectral, cols_table, precision=highest)
    spectral = spectral / eigen_table(NX, NY)
    spatial = jnp.einsum('xp,mpq->mxq', rows_table, spectral, precision=highest)
    return jnp.einsum('mxq,qy->mxy', spatial, cols_table, precision=highest)

def reference(guess, right_side, mean_coef, field_coef, coupling, coupling_list, pair_count):
    highest = lax.Precision.HIGHEST
    coef_rows = jnp.pad(mean_coef, ((1, 1), (0, 0)), mode='edge')
    field_rows = jnp.pad(field_coef, ((0, 0), (1, 1), (0, 0)), mode='edge')
    solution = guess
    residual = right_side
    for sweep in range(ITERS):
        padded = jnp.pad(solution, ((0, 0), (1, 1), (0, 0)))
        mean_part = operate(padded, coef_rows)
        state = solution.astype(jnp.bfloat16).reshape(BLOCKS, BLK, NX * NY)

        def block_term(index):
            entries = coupling_list[index]
            partner = (entries // FIELDS).astype(jnp.int32)
            field_index = (entries % FIELDS).astype(jnp.int32)
            live_mask = jnp.arange(MAXC).astype(jnp.int32) < pair_count[index]
            onehot = ((field_index[:, None] == jnp.arange(FIELDS).astype(jnp.int32)[None, :]) & live_mask[:, None]).astype(jnp.float32)
            gathered = state[partner].astype(jnp.float32)
            products = jnp.einsum('kab,kbc->kac', coupling[index].astype(jnp.float32), gathered, precision=highest)
            grouped = jnp.einsum('kf,kac->fac', onehot, products, precision=highest).reshape(FIELDS, BLK, NX, NY)
            grouped_pad = jnp.pad(grouped, ((0, 0), (0, 0), (1, 1), (0, 0)))
            return lax.optimization_barrier(jnp.sum(operate(grouped_pad, field_rows[:, None]), axis=0))
        coupled = lax.map(block_term, jnp.arange(BLOCKS).astype(jnp.int32)).reshape(MODES, NX, NY)
        residual = right_side - mean_part - coupled
        solution = solution + relaxation * mean_solve(residual)
    return (solution, residual)
```

```python
import functools
import math

import jax
import jax.numpy as jnp
import numpy as np
from jax import lax
from jax.experimental import pallas as pl
from jax.experimental.pallas import tpu as pltpu
from jax.sharding import PartitionSpec as P

FIELDS = 3
MAXC = 16
BLK = 128
ITERS = 2
RELAX = 0.6
F32 = jnp.float32
BF16 = jnp.bfloat16


LOW_ROWS = 8
LOW_COLS = 16


def halves(table):
    hi = np.asarray(table, np.float32).astype(BF16)
    lo = (np.asarray(table, np.float32) - hi.astype(np.float32)).astype(BF16)
    return hi, lo, np.zeros_like(hi)


def fore_table(sine):
    hi, lo, zero = halves(sine)
    low = np.tile(hi[:, :LOW_COLS], (1, LOW_ROWS))
    return np.concatenate(
        [np.concatenate([hi, lo, low], 1), np.concatenate([hi, zero, zero], 1)], 0
    )


def back_table(sine):
    hi, lo, zero = halves(sine)
    low = np.tile(hi[:LOW_COLS], (LOW_ROWS, 1))
    return np.concatenate(
        [
            np.concatenate([hi, lo], 1),
            np.concatenate([hi, zero], 1),
            np.concatenate([low, zero], 1),
        ],
        0,
    )


def single(length):
    f32 = np.float32
    counter = np.arange(length).astype(f32) + f32(1.0)
    angle = f32(math.pi) * counter[:, None] * counter[None] / f32(length + 1)
    sine = np.sin(angle.astype(np.float64)).astype(f32)
    sine = f32(math.sqrt(2.0 / (length + 1))) * sine
    turn = f32(math.pi) * counter / f32(length + 1)
    return sine, f32(2.0) * np.cos(turn.astype(np.float64)).astype(f32)


def tables(rows, cols, slabs):
    length = rows * slabs
    sine, along = single(cols)
    across = single(length)[1]
    diag = 4.0 - along.astype(np.float64)
    pivot = np.zeros((rows, cols))
    pivot[0] = 1.0 / diag
    for x in range(1, rows):
        pivot[x] = 1.0 / (diag - pivot[x - 1])
    reach = np.cumprod(pivot, axis=0)
    first = np.zeros((rows, cols))
    meet = np.zeros((slabs, 2, 2 * slabs, cols))
    eye = np.eye(rows)
    shift = np.eye(rows, k=1) + np.eye(rows, k=-1)
    for q in range(cols):
        column = np.linalg.solve(diag[q] * eye - shift, eye[0])
        first[:, q] = column
        near, far = column[0], column[-1]
        system = np.eye(2 * slabs)
        for s in range(slabs):
            if s > 0:
                system[s, slabs + s - 1] -= near
                system[slabs + s, slabs + s - 1] -= far
            if s < slabs - 1:
                system[s, s + 1] -= far
                system[slabs + s, s + 1] -= near
        inverse = np.linalg.inv(system)
        for s in range(slabs):
            if s > 0:
                meet[s, 0, :, q] = inverse[slabs + s - 1]
            if s < slabs - 1:
                meet[s, 1, :, q] = inverse[s + 1]
    p = np.arange(LOW_ROWS)
    rounded = (np.float32(4.0) - across[:LOW_ROWS, None]) - along[None, :LOW_COLS]
    smooth = diag[None, :LOW_COLS] - 2.0 * np.cos(np.pi * (p + 1.0) / (length + 1))[:, None]
    gap = 1.0 / rounded.astype(np.float64) - 1.0 / smooth
    gap = np.broadcast_to(gap.reshape(1, cols), (8, cols)).astype(np.float32)
    place = np.arange(slabs)[:, None] * rows + np.arange(rows + 2)[None]
    waves = np.sqrt(2.0 / (length + 1)) * np.sin(
        np.pi * place[:, :, None] * (p + 1.0) / (length + 1)
    )
    waves = np.repeat(waves, LOW_COLS, axis=2)
    waves = np.broadcast_to(waves[:, :, None], (slabs, rows + 2, 8, cols)).astype(np.float32)
    sweep = np.stack([pivot, first, reach])
    sweep = np.broadcast_to(sweep[:, :, None], (3, rows, 8, cols)).astype(np.float32)
    meet = np.broadcast_to(meet[:, :, :, None], (slabs, 2, 2 * slabs, 8, cols)).astype(np.float32)
    return sine, sweep, meet, waves, gap


def tiled(plane):
    return plane.reshape(plane.shape[0] // 8, 8, plane.shape[1])


def flat(plane):
    return plane.reshape(plane.shape[0] * 8, plane.shape[2])


def transform(plane, table, extra=None):
    hi = plane.astype(BF16)
    lo = (plane - hi.astype(F32)).astype(BF16)
    parts = [hi, lo] if extra is None else [hi, lo, extra]
    both = jnp.dot(jnp.concatenate(parts, 1), table, preferred_element_type=F32)
    cols = plane.shape[1]
    return both[:, :cols] + both[:, cols : 2 * cols], both[:, 2 * cols :]


def averages(center, above, below):
    cols = center.shape[1]
    lane = lax.broadcasted_iota(jnp.int32, center.shape, 1)
    left = 0.5 * (center + pltpu.roll(center, 1, 1))
    right = 0.5 * (center + pltpu.roll(center, cols - 1, 1))
    up = 0.5 * (center + above)
    down = 0.5 * (center + below)
    zero = jnp.zeros_like(center)
    total = (
        up + down + jnp.where(lane == 0, center, left) + jnp.where(lane == cols - 1, center, right)
    )
    return (
        total,
        jnp.where(lane == 0, zero, left),
        jnp.where(lane == cols - 1, zero, right),
        up,
        down,
    )


def body(
    D,
    NS,
    R,
    list_s,
    count_s,
    guess_h,
    right_h,
    mean_v,
    field_v,
    coup_h,
    fore_v,
    back_v,
    sweep_v,
    meet_v,
    waves_v,
    gap_v,
    sol_h,
    res_h,
    stage_g,
    stage_b,
    stage_r,
    coup_v,
    u,
    sb,
    r0,
    rh,
    strips,
    images,
    outb,
    cin,
    ex,
    low,
    low_ex,
    edge,
    edge_in,
    cpad,
    mco,
    fco,
    lsem,
    hs,
    hr,
    fs,
    fr,
    ps,
    pr,
    os_,
    or_,
    xs,
    xr,
    zs,
    zr,
):
    D2 = D // 2
    N = BLK
    cols = guess_h.shape[1]
    d = lax.axis_index("mode")
    s = lax.axis_index("slab")
    C = d // 2
    p = d % 2
    partner = 2 * C + 1 - p
    above = (s + NS - 1) % NS
    below = (s + 1) % NS
    CH = 32

    def remote(src, dst, send, recv, mode, slab):
        return pltpu.make_async_remote_copy(
            src_ref=src,
            dst_ref=dst,
            send_sem=send,
            recv_sem=recv,
            device_id=(mode, slab),
            device_id_type=pl.DeviceIdType.MESH,
        )

    def landed(ref, sem):
        pltpu.make_async_copy(ref, ref, sem).wait()

    load_g = pltpu.make_async_copy(guess_h, stage_g, lsem.at[0])
    load_b = pltpu.make_async_copy(right_h, stage_b, lsem.at[1])
    load_c = pltpu.make_async_copy(coup_h, coup_v, lsem.at[2])
    load_g.start()
    load_b.start()
    load_c.start()

    barrier = pltpu.get_barrier_semaphore()

    @pl.loop(1, D)
    def _(t):
        pl.semaphore_signal(
            barrier, inc=1, device_id=((d + t) % D, s), device_id_type=pl.DeviceIdType.MESH
        )

    @pl.loop(1, NS)
    def _(t):
        pl.semaphore_signal(
            barrier, inc=1, device_id=(d, (s + t) % NS), device_id_type=pl.DeviceIdType.MESH
        )

    for f in range(FIELDS + 1):
        whole = mean_v[...] if f == 0 else field_v[f - 1]
        cpad[f, pl.ds(8, R), :] = whole
        edge[0, pl.ds(f, 1), :] = whole[:1]
        edge[1, pl.ds(f, 1), :] = whole[R - 1 :]
    images[3 * D] = jnp.zeros((N, 2 * cols), BF16)
    pl.semaphore_wait(barrier, D - 1 + NS - 1)

    coef_up = remote(edge.at[0], edge_in.at[1], hs.at[2], hr.at[2], d, above)
    coef_down = remote(edge.at[1], edge_in.at[0], hs.at[3], hr.at[3], d, below)
    coef_up.start()
    coef_down.start()
    load_g.wait()

    def take(x):
        plane = stage_g[pl.ds(x, N, stride=R), :]
        u[x + 1] = plane
        sb[x + 1] = plane.astype(BF16)

    take(0)
    take(R - 1)
    halo_up = remote(u.at[1], u.at[R + 1], hs.at[0], hr.at[0], d, above)
    halo_down = remote(u.at[R], u.at[0], hs.at[1], hr.at[1], d, below)
    halo_up.start()
    halo_down.start()

    def send_pair(it, i):
        for live, j, half in ((i < D2, 2 * i, 0), (i >= 1, 2 * i - 1, 1)):
            source = sb.at[pl.ds(2 * i, 2)]
            target = strips.at[it, d, pl.ds(2 * half, 2)]

            @pl.when(jnp.logical_and(live, j != d))
            def _():
                remote(source, target, fs.at[it, j], fr.at[it, d], j, s).start()

            @pl.when(jnp.logical_and(live, j == d))
            def _():
                pltpu.make_async_copy(source, target, fr.at[it, d]).start()

    def sent_pairs(it):
        @pl.loop(1, D)
        def _(t):
            j = (d + t) % D
            remote(
                sb.at[pl.ds(0, 2)], strips.at[it, d, pl.ds(0, 2)], fs.at[it, j], fr.at[it, d], j, s
            ).wait_send()

    @pl.loop(0, D2 - 1)
    def _(k):
        i = 1 + (C + k) % (D2 - 1)

        @pl.loop(0, 2)
        def _(h):
            take(2 * i + h - 1)

        send_pair(0, i)

    coef_up.wait()
    coef_down.wait()
    for f in range(FIELDS + 1):
        whole = cpad[f, pl.ds(8, R), :]
        cpad[f, pl.ds(7, 1), :] = jnp.where(s == 0, whole[:1], edge_in[0, pl.ds(f, 1), :])
        cpad[f, pl.ds(8 + R, 1), :] = jnp.where(
            s == NS - 1, whole[R - 1 :], edge_in[1, pl.ds(f, 1), :]
        )
    halo_up.wait()
    halo_down.wait()
    top = jnp.where(s == 0, jnp.zeros((N, cols), F32), u[0])
    bottom = jnp.where(s == NS - 1, jnp.zeros((N, cols), F32), u[R + 1])
    u[0] = top
    u[R + 1] = bottom
    sb[0] = top.astype(BF16)
    sb[R + 1] = bottom.astype(BF16)
    send_pair(0, 0)
    send_pair(0, D2)

    for n, value in enumerate(
        averages(cpad[0, pl.ds(8, R), :], cpad[0, pl.ds(7, R), :], cpad[0, pl.ds(9, R), :])
    ):
        mco[n] = jnp.broadcast_to(value[:, None, :], (R, 8, cols))
    for f in range(FIELDS):
        rows3 = [
            jnp.broadcast_to(cpad[f + 1, pl.ds(7 + d + n, 1), :], (8, cols)) for n in range(3)
        ]
        for n, value in enumerate(averages(rows3[1], rows3[0], rows3[2])):
            fco[f, n] = value
    load_b.wait()
    load_c.wait()

    def apply_mean(x):
        co = [mco[n, x] for n in range(5)]
        for m in range(0, N, CH):
            mid = u[x + 1, pl.ds(m, CH), :]
            left = pltpu.roll(mid, 1, 1)
            right = pltpu.roll(mid, cols - 1, 1)
            total = co[0] * tiled(mid) - co[1] * tiled(left) - co[2] * tiled(right)
            total = total - co[3] * tiled(u[x, pl.ds(m, CH), :])
            total = total - co[4] * tiled(u[x + 2, pl.ds(m, CH), :])
            side = stage_b[pl.ds(m * R + x, CH, stride=R), :]
            r0[x, pl.ds(m, CH), :] = side - flat(total)

    def make_images(it, src):
        for m in range(0, N, CH):
            up, mid, down = (
                strips[it, src, p + n, pl.ds(m, CH), :].astype(F32) for n in range(3)
            )
            left = tiled(pltpu.roll(mid, 1, 1))
            right = tiled(pltpu.roll(mid, cols - 1, 1))
            up, mid, down = tiled(up), tiled(mid), tiled(down)
            for f in range(FIELDS):
                value = flat(
                    fco[f, 0] * mid
                    - fco[f, 1] * left
                    - fco[f, 2] * right
                    - fco[f, 3] * up
                    - fco[f, 4] * down
                )
                hi = value.astype(BF16)
                lo = (value - hi.astype(F32)).astype(BF16)
                images[3 * src + f, pl.ds(m, CH), :cols] = hi
                images[3 * src + f, pl.ds(m, CH), cols:] = lo

    for it in range(ITERS):
        last = it == ITERS - 1

        @pl.loop(0, R)
        def _(x):
            apply_mean(x)

        def source_at(t):
            return 2 * ((C + D2 - t // 2) % D2) + t % 2

        def relay(t):
            src = source_at(t)
            shared = strips.at[it, src, 1 + p]
            return remote(shared, shared, ps.at[it, src], pr.at[it, src], partner, s)

        LAG = 2

        @pl.loop(0, D + LAG)
        def _(t):
            @pl.when(t < D)
            def _():
                src = source_at(t)
                landed(strips.at[it, src, pl.ds(2 * p, 2)], fr.at[it, src])
                relay(t).start()

            @pl.when(t >= LAG)
            def _():
                before = t - LAG
                relay(before).wait_recv()
                make_images(it, source_at(before))

        @pl.loop(0, D)
        def _(t):
            relay(t).wait_send()

        sent_pairs(it)

        def result(i):
            return remote(
                outb.at[it, i], cin.at[it, d], os_.at[it, i], or_.at[it, d], i, s
            )

        @pl.loop(0, D)
        def _(t):
            i = 2 * ((C + 1 + t // 2) % D2) + t % 2
            count = count_s[i]
            lefts = []
            rights = []
            for k in range(MAXC):
                entry = jnp.where(k < count, list_s[i * MAXC + k], 3 * D)
                lefts.append(coup_v[i, k])
                rights.append(images[entry])
            both = jnp.dot(
                jnp.concatenate(lefts, 1),
                jnp.concatenate(rights, 0),
                preferred_element_type=F32,
            )
            outb[it, i] = both[:, :cols] + both[:, cols:]

            @pl.when(i != d)
            def _():
                result(i).start()

            @pl.when(i == d)
            def _():
                pltpu.make_async_copy(outb.at[it, i], cin.at[it, d], or_.at[it, d]).start()

        if not last:
            low[...] = jnp.zeros((N, cols), F32)

        @pl.loop(0, D)
        def _(t):
            x = 2 * ((C + D2 - 1 - t // 2) % D2) + t % 2
            landed(cin.at[it, x], or_.at[it, x])
            plane = r0[x] - cin[it, x]
            if last:
                stage_r[pl.ds(x, N, stride=R), :] = plane
            if last:
                rh[x + 1] = transform(plane, fore_v[:, pl.ds(0, 2 * cols)])[0]
            else:
                rh[x + 1], part = transform(plane, fore_v[...])
                low[...] += flat(tiled(part) * waves_v[s, x + 1])

        @pl.loop(1, D)
        def _(t):
            result((d + t) % D).wait_send()

        if last:
            store_r = pltpu.make_async_copy(stage_r, res_h, lsem.at[3])
            store_r.start()

        @pl.loop(0, N // CH)
        def _(c):
            m = pl.multiple_of(c * CH, CH)
            ms = pl.ds(m, CH)
            run = jnp.zeros((CH // 8, 8, cols), F32)
            head = jnp.zeros((CH // 8, 8, cols), F32)
            for x in range(R):
                value = tiled(rh[x + 1, ms, :])
                head = head + sweep_v[1, x] * value
                run = (run + value) * sweep_v[0, x]
                rh[x + 1, ms, :] = flat(run)
            ex[it, s, 0, ms, :] = flat(head)
            ex[it, s, 1, ms, :] = flat(run)

        def swap(t):
            mine = ex.at[it, s]
            return remote(mine, mine, xs.at[it, t], xr.at[it, s], d, (s + t) % NS)

        def swap_low(t):
            mine = low_ex.at[s]
            return remote(mine, mine, zs.at[t], zr.at[s], d, (s + t) % NS)

        if not last:
            low_ex[s] = low[...].astype(BF16)

        @pl.loop(1, NS)
        def _(t):
            swap(t).start()
            if not last:
                swap_low(t).start()

        @pl.loop(1, NS)
        def _(t):
            other = (s + t) % NS
            landed(ex.at[it, other], xr.at[it, other])
            if not last:
                landed(low_ex.at[other], zr.at[other])

        @pl.loop(0, N // CH)
        def _(c):
            m = pl.multiple_of(c * CH, CH)
            ms = pl.ds(m, CH)
            ends = [tiled(ex[it, k % NS, k // NS, ms, :]) for k in range(2 * NS)]
            outer = []
            for side in range(2):
                total = meet_v[s, side, 0] * ends[0]
                for k in range(1, 2 * NS):
                    total = total + meet_v[s, side, k] * ends[k]
                outer.append(total)
            rh[0, ms, :] = flat(outer[0])
            rh[R + 1, ms, :] = flat(outer[1])
            run = outer[1]
            for x in reversed(range(R)):
                run = tiled(rh[x + 1, ms, :]) + sweep_v[2, x] * outer[0] + sweep_v[0, x] * run
                rh[x + 1, ms, :] = flat(run)

        @pl.loop(1, NS)
        def _(t):
            swap(t).wait_send()
            if not last:
                swap_low(t).wait_send()

        if last:

            @pl.loop(0, R)
            def _(x):
                plane = u[x + 1] + transform(rh[x + 1], back_v[pl.ds(0, 2 * cols), :])[0]
                stage_g[pl.ds(x, N, stride=R), :] = plane

        else:
            total = low_ex[0].astype(F32)
            for k in range(1, NS):
                total = total + low_ex[k].astype(F32)
            low[...] = flat(tiled(total) * gap_v[...])

            @pl.loop(0, D2 + 1)
            def _(k):
                i = (C + k) % (D2 + 1)

                @pl.loop(0, 2)
                def _(h):
                    x = 2 * i + h
                    wave = flat(tiled(low[...]) * waves_v[s, x]).astype(BF16)
                    plane = u[x] + transform(rh[x], back_v[...], wave)[0]
                    u[x] = plane
                    sb[x] = plane.astype(BF16)

                send_pair(it + 1, i)

    store_s = pltpu.make_async_copy(stage_g, sol_h, lsem.at[4])
    store_s.start()
    store_r.wait()
    store_s.wait()


def local(D, NS, interpret, guess, right_side, mean_coef, field_coef, coupling, listed, count):
    modes, R, cols = guess.shape
    N = BLK
    sine, sweep, meet, waves, gap = tables(R, cols, NS)
    fore = fore_table(sine)
    back = back_table(RELAX * sine.astype(np.float64))
    flat_shape = jax.ShapeDtypeStruct((modes * R, cols), F32)
    hbm = pl.BlockSpec(memory_space=pl.ANY)
    vmem = pl.BlockSpec(memory_space=pltpu.VMEM)
    smem = pl.BlockSpec(memory_space=pltpu.SMEM)
    sems = pltpu.SemaphoreType.DMA
    sol, res = pl.pallas_call(
        functools.partial(body, D, NS, R),
        out_shape=(flat_shape, flat_shape),
        in_specs=[smem, smem, hbm, hbm, vmem, vmem, hbm] + [vmem] * 6,
        out_specs=(hbm, hbm),
        scratch_shapes=[
            pltpu.VMEM((modes * R, cols), F32),
            pltpu.VMEM((modes * R, cols), F32),
            pltpu.VMEM((modes * R, cols), F32),
            pltpu.VMEM((D, MAXC, N, N), BF16),
            pltpu.VMEM((R + 2, N, cols), F32),
            pltpu.VMEM((R + 2, N, cols), BF16),
            pltpu.VMEM((R, N, cols), F32),
            pltpu.VMEM((R + 2, N, cols), F32),
            pltpu.VMEM((ITERS, D, 4, N, cols), BF16),
            pltpu.VMEM((FIELDS * D + 1, N, 2 * cols), BF16),
            pltpu.VMEM((ITERS, D, N, cols), F32),
            pltpu.VMEM((ITERS, R, N, cols), F32),
            pltpu.VMEM((ITERS, NS, 2, N, cols), F32),
            pltpu.VMEM((N, cols), F32),
            pltpu.VMEM((NS, N, cols), BF16),
            pltpu.VMEM((2, 8, cols), F32),
            pltpu.VMEM((2, 8, cols), F32),
            pltpu.VMEM((FIELDS + 1, R + 16, cols), F32),
            pltpu.VMEM((5, R, 8, cols), F32),
            pltpu.VMEM((FIELDS, 5, 8, cols), F32),
            sems((5,)),
            sems((4,)),
            sems((4,)),
            sems((ITERS, D)),
            sems((ITERS, D)),
            sems((ITERS, D)),
            sems((ITERS, D)),
            sems((ITERS, D)),
            sems((ITERS, D)),
            sems((ITERS, NS)),
            sems((ITERS, NS)),
            sems((NS,)),
            sems((NS,)),
        ],
        compiler_params=pltpu.CompilerParams(
            collective_id=0, has_side_effects=True, vmem_limit_bytes=67043328
        ),
        interpret=interpret,
    )(
        listed.reshape(-1),
        count,
        guess.reshape(modes * R, cols),
        right_side.reshape(modes * R, cols),
        mean_coef,
        field_coef,
        coupling,
        *(jnp.asarray(table) for table in (fore, back, sweep, meet, waves, gap)),
    )
    return sol.reshape(guess.shape), res.reshape(guess.shape)


def solution(mesh, interpret=False):
    placed = (
        P("mode", "slab", None),
        P("mode", "slab", None),
        P("slab", None),
        P(None, "slab", None),
        P(),
        P(),
        P(),
    )
    return jax.shard_map(
        functools.partial(local, mesh.shape["mode"], mesh.shape["slab"], interpret),
        mesh=mesh,
        in_specs=placed,
        out_specs=(P("mode", "slab", None), P("mode", "slab", None)),
        check_vma=False,
    )
```

```python
import functools
import math

import jax
import jax.numpy as jnp
import numpy as np
from jax import lax
from jax.experimental import pallas as pl
from jax.experimental.pallas import tpu as pltpu
from jax.sharding import PartitionSpec as P

FIELDS = 3
MAXC = 16
BLK = 128
ITERS = 2
RELAX = 0.6
STEPS = 32760.0
F32 = jnp.float32
BF16 = jnp.bfloat16


LOW_ROWS = 8
LOW_COLS = 16


def halves(table):
    hi = np.asarray(table, np.float32).astype(BF16)
    lo = (np.asarray(table, np.float32) - hi.astype(np.float32)).astype(BF16)
    return hi, lo, np.zeros_like(hi)


def fore_table(sine):
    hi, lo, zero = halves(sine)
    low = np.tile(hi[:, :LOW_COLS], (1, LOW_ROWS))
    return np.concatenate(
        [np.concatenate([hi, lo, low], 1), np.concatenate([hi, zero, zero], 1)], 0
    )


def back_table(sine):
    hi, lo, zero = halves(sine)
    low = np.tile(hi[:LOW_COLS], (LOW_ROWS, 1))
    return np.concatenate(
        [
            np.concatenate([hi, lo], 1),
            np.concatenate([hi, zero], 1),
            np.concatenate([low, zero], 1),
        ],
        0,
    )


def single(length):
    f32 = np.float32
    counter = np.arange(length).astype(f32) + f32(1.0)
    angle = f32(math.pi) * counter[:, None] * counter[None] / f32(length + 1)
    sine = np.sin(angle.astype(np.float64)).astype(f32)
    sine = f32(math.sqrt(2.0 / (length + 1))) * sine
    turn = f32(math.pi) * counter / f32(length + 1)
    return sine, f32(2.0) * np.cos(turn.astype(np.float64)).astype(f32)


def tables(rows, cols, slabs):
    length = rows * slabs
    sine, along = single(cols)
    across = single(length)[1]
    diag = 4.0 - along.astype(np.float64)
    pivot = np.zeros((rows, cols))
    pivot[0] = 1.0 / diag
    for x in range(1, rows):
        pivot[x] = 1.0 / (diag - pivot[x - 1])
    reach = np.cumprod(pivot, axis=0)
    first = np.zeros((rows, cols))
    meet = np.zeros((slabs, 2, 2 * slabs, cols))
    eye = np.eye(rows)
    shift = np.eye(rows, k=1) + np.eye(rows, k=-1)
    for q in range(cols):
        column = np.linalg.solve(diag[q] * eye - shift, eye[0])
        first[:, q] = column
        near, far = column[0], column[-1]
        system = np.eye(2 * slabs)
        for s in range(slabs):
            if s > 0:
                system[s, slabs + s - 1] -= near
                system[slabs + s, slabs + s - 1] -= far
            if s < slabs - 1:
                system[s, s + 1] -= far
                system[slabs + s, s + 1] -= near
        inverse = np.linalg.inv(system)
        for s in range(slabs):
            if s > 0:
                meet[s, 0, :, q] = inverse[slabs + s - 1]
            if s < slabs - 1:
                meet[s, 1, :, q] = inverse[s + 1]
    p = np.arange(LOW_ROWS)
    rounded = (np.float32(4.0) - across[:LOW_ROWS, None]) - along[None, :LOW_COLS]
    smooth = diag[None, :LOW_COLS] - 2.0 * np.cos(np.pi * (p + 1.0) / (length + 1))[:, None]
    gap = 1.0 / rounded.astype(np.float64) - 1.0 / smooth
    gap = np.broadcast_to(gap.reshape(1, cols), (8, cols)).astype(np.float32)
    place = np.arange(slabs)[:, None] * rows + np.arange(rows + 2)[None]
    waves = np.sqrt(2.0 / (length + 1)) * np.sin(
        np.pi * place[:, :, None] * (p + 1.0) / (length + 1)
    )
    waves = np.repeat(waves, LOW_COLS, axis=2)
    waves = np.broadcast_to(waves[:, :, None], (slabs, rows + 2, 8, cols)).astype(np.float32)
    sweep = np.stack([pivot, first, reach])
    sweep = np.broadcast_to(sweep[:, :, None], (3, rows, 8, cols)).astype(np.float32)
    meet = np.broadcast_to(meet[:, :, :, None], (slabs, 2, 2 * slabs, 8, cols)).astype(np.float32)
    return sine, sweep, meet, waves, gap


def tiled(plane):
    return plane.reshape(plane.shape[0] // 8, 8, plane.shape[1])


def flat(plane):
    return plane.reshape(plane.shape[0] * 8, plane.shape[2])


def transform(plane, table, extra=None):
    hi = plane.astype(BF16)
    lo = (plane - hi.astype(F32)).astype(BF16)
    parts = [hi, lo] if extra is None else [hi, lo, extra]
    both = jnp.dot(jnp.concatenate(parts, 1), table, preferred_element_type=F32)
    cols = plane.shape[1]
    return both[:, :cols] + both[:, cols : 2 * cols], both[:, 2 * cols :]


def averages(center, above, below):
    cols = center.shape[1]
    lane = lax.broadcasted_iota(jnp.int32, center.shape, 1)
    left = 0.5 * (center + pltpu.roll(center, 1, 1))
    right = 0.5 * (center + pltpu.roll(center, cols - 1, 1))
    up = 0.5 * (center + above)
    down = 0.5 * (center + below)
    zero = jnp.zeros_like(center)
    total = (
        up + down + jnp.where(lane == 0, center, left) + jnp.where(lane == cols - 1, center, right)
    )
    return (
        total,
        jnp.where(lane == 0, zero, left),
        jnp.where(lane == cols - 1, zero, right),
        up,
        down,
    )


def body(
    D,
    NS,
    R,
    list_s,
    count_s,
    guess_h,
    right_h,
    mean_v,
    field_v,
    coup_h,
    fore_h,
    back_h,
    sweep_h,
    meet_h,
    waves_h,
    gap_v,
    sol_h,
    res_h,
    stage_g,
    stage_b,
    fore_v,
    back_v,
    sweep_v,
    meet_v,
    waves_v,
    coup_v,
    u,
    sb,
    r0,
    rh,
    strips,
    images,
    outq,
    outs,
    inq,
    ins,
    ex,
    low,
    low_ex,
    edge,
    edge_in,
    cpad,
    mco,
    fco,
    lsem,
    hs,
    hr,
    fs,
    fr,
    ps,
    pr,
    os_,
    or_,
    xs,
    xr,
    zs,
    zr,
    table_sem,
    coup_sem,
):
    D2 = D // 2
    N = BLK
    cols = guess_h.shape[1]
    WINDOW = min(4, D2 - 1)
    d = lax.axis_index("mode")
    s = lax.axis_index("slab")
    C = d // 2
    p = d % 2
    partner = 2 * C + 1 - p
    above = (s + NS - 1) % NS
    below = (s + 1) % NS
    CH = 32

    def remote(src, dst, send, recv, mode, slab):
        return pltpu.make_async_remote_copy(
            src_ref=src,
            dst_ref=dst,
            send_sem=send,
            recv_sem=recv,
            device_id=(mode, slab),
            device_id_type=pl.DeviceIdType.MESH,
        )

    def landed(ref, sem):
        pltpu.make_async_copy(ref, ref, sem).wait()

    HM = N // 2
    load_g = pltpu.make_async_copy(guess_h, stage_g, lsem.at[0])
    load_b = pltpu.make_async_copy(right_h, stage_b, lsem.at[1])
    load_g.start()

    def load_coupling(k):
        some = pl.ds(2 * k, 2)
        return pltpu.make_async_copy(coup_h.at[some], coup_v.at[some], coup_sem.at[k])

    table_loads = [
        pltpu.make_async_copy(source, target, table_sem.at[n])
        for n, (source, target) in enumerate(
            (
                (fore_h, fore_v),
                (back_h, back_v),
                (sweep_h, sweep_v),
                (meet_h.at[s], meet_v),
                (waves_h.at[s], waves_v),
            )
        )
    ]

    barrier = pltpu.get_barrier_semaphore()

    @pl.loop(1, D)
    def _(t):
        pl.semaphore_signal(
            barrier, inc=1, device_id=((d + t) % D, s), device_id_type=pl.DeviceIdType.MESH
        )

    @pl.loop(1, NS)
    def _(t):
        pl.semaphore_signal(
            barrier, inc=1, device_id=(d, (s + t) % NS), device_id_type=pl.DeviceIdType.MESH
        )

    for f in range(FIELDS + 1):
        whole = mean_v[...] if f == 0 else field_v[f - 1]
        cpad[f, pl.ds(8, R), :] = whole
        edge[0, pl.ds(f, 1), :] = whole[:1]
        edge[1, pl.ds(f, 1), :] = whole[R - 1 :]
    images[3 * D] = jnp.zeros((N, 2 * cols), BF16)
    load_g.wait()

    def take(x):
        plane = stage_g[pl.ds(x, N, stride=R), :]
        u[x + 1] = plane
        sb[x + 1] = plane.astype(BF16)

    take(0)
    take(R - 1)
    pl.semaphore_wait(barrier, D - 1 + NS - 1)

    halo_up = remote(u.at[1], u.at[R + 1], hs.at[0], hr.at[0], d, above)
    halo_down = remote(u.at[R], u.at[0], hs.at[1], hr.at[1], d, below)
    coef_up = remote(edge.at[0], edge_in.at[1], hs.at[2], hr.at[2], d, above)
    coef_down = remote(edge.at[1], edge_in.at[0], hs.at[3], hr.at[3], d, below)
    halo_up.start()
    halo_down.start()
    coef_up.start()
    coef_down.start()

    def pair_copies(it, i, g):
        source = sb.at[pl.ds(2 * i, 2), pl.ds(g * HM, HM)]
        for live, j, half in ((i < D2, 2 * i, 0), (i >= 1, 2 * i - 1, 1)):
            target = strips.at[it, d, pl.ds(2 * half, 2), pl.ds(g * HM, HM)]
            yield live, j, source, target

    def send_pair(it, i, g):
        for live, j, source, target in pair_copies(it, i, g):

            @pl.when(jnp.logical_and(live, j != d))
            def _():
                remote(source, target, fs.at[it, g, j], fr.at[it, g, d], j, s).start()

            @pl.when(jnp.logical_and(live, j == d))
            def _():
                pltpu.make_async_copy(source, target, fr.at[it, g, d]).start()

    def sent_pairs(it):
        @pl.loop(1, D)
        def _(t):
            j = (d + t) % D
            for g in range(2):
                source = sb.at[pl.ds(0, 2), pl.ds(g * HM, HM)]
                target = strips.at[it, d, pl.ds(0, 2), pl.ds(g * HM, HM)]
                remote(source, target, fs.at[it, g, j], fr.at[it, g, d], j, s).wait_send()

    def pair_at(it, k):
        return 1 + (C + D2 - 2 + k) % (D2 - 1) if it == 0 else (C + k) % (D2 + 1)

    def pairs(it):
        return D2 - 1 if it == 0 else D2 + 1

    def take_pair(k):
        i = pair_at(0, k)
        for h in range(2):
            x = 2 * i + h - 1

            @pl.when(jnp.logical_and(x != 0, x != R - 1))
            def _():
                take(x)

    @pl.loop(0, WINDOW)
    def _(k):
        take_pair(k)
        for g in range(2):
            send_pair(0, pair_at(0, k), g)

    load_b.start()
    for copy in table_loads:
        copy.start()

    @pl.loop(WINDOW, D2 - 1)
    def _(k):
        take_pair(k)

    coef_up.wait()
    coef_down.wait()
    for f in range(FIELDS + 1):
        whole = cpad[f, pl.ds(8, R), :]
        cpad[f, pl.ds(7, 1), :] = jnp.where(s == 0, whole[:1], edge_in[0, pl.ds(f, 1), :])
        cpad[f, pl.ds(8 + R, 1), :] = jnp.where(
            s == NS - 1, whole[R - 1 :], edge_in[1, pl.ds(f, 1), :]
        )
    halo_up.wait()
    halo_down.wait()
    top = jnp.where(s == 0, jnp.zeros((N, cols), F32), u[0])
    bottom = jnp.where(s == NS - 1, jnp.zeros((N, cols), F32), u[R + 1])
    u[0] = top
    u[R + 1] = bottom
    sb[0] = top.astype(BF16)
    sb[R + 1] = bottom.astype(BF16)
    for g in range(2):
        send_pair(0, 0, g)
        send_pair(0, D2, g)

    for n, value in enumerate(
        averages(cpad[0, pl.ds(8, R), :], cpad[0, pl.ds(7, R), :], cpad[0, pl.ds(9, R), :])
    ):
        mco[n] = jnp.broadcast_to(value[:, None, :], (R, 8, cols))
    for f in range(FIELDS):
        rows3 = [
            jnp.broadcast_to(cpad[f + 1, pl.ds(7 + d + n, 1), :], (8, cols)) for n in range(3)
        ]
        for n, value in enumerate(averages(rows3[1], rows3[0], rows3[2])):
            fco[f, n] = value
    load_b.wait()
    for copy in table_loads:
        copy.wait()

    def apply_mean(x):
        co = [mco[n, x] for n in range(5)]
        for m in range(0, N, CH):
            mid = u[x + 1, pl.ds(m, CH), :]
            left = pltpu.roll(mid, 1, 1)
            right = pltpu.roll(mid, cols - 1, 1)
            total = co[0] * tiled(mid) - co[1] * tiled(left) - co[2] * tiled(right)
            total = total - co[3] * tiled(u[x, pl.ds(m, CH), :])
            total = total - co[4] * tiled(u[x + 2, pl.ds(m, CH), :])
            side = stage_b[pl.ds(m * R + x, CH, stride=R), :]
            r0[x, pl.ds(m, CH), :] = side - flat(total)

    def make_images(it, src):
        for m in range(0, N, CH):
            up, mid, down = (
                strips[it, src, p + n, pl.ds(m, CH), :].astype(F32) for n in range(3)
            )
            left = tiled(pltpu.roll(mid, 1, 1))
            right = tiled(pltpu.roll(mid, cols - 1, 1))
            up, mid, down = tiled(up), tiled(mid), tiled(down)
            for f in range(FIELDS):
                value = flat(
                    fco[f, 0] * mid
                    - fco[f, 1] * left
                    - fco[f, 2] * right
                    - fco[f, 3] * up
                    - fco[f, 4] * down
                )
                hi = value.astype(BF16)
                lo = (value - hi.astype(F32)).astype(BF16)
                images[3 * src + f, pl.ds(m, CH), :cols] = hi
                images[3 * src + f, pl.ds(m, CH), cols:] = lo

    for it in range(ITERS):
        last = it == ITERS - 1

        def source_at(k, q):
            return 2 * ((C + D2 - k) % D2) + q

        def relay(k, q):
            src = source_at(k, q)
            shared = strips.at[it, src, 1 + p]
            return remote(shared, shared, ps.at[it, src], pr.at[it, src], partner, s)

        def arrive(k):
            for q in range(2):
                src = source_at(k, q)
                for g in range(2):
                    landed(
                        strips.at[it, src, pl.ds(2 * p, 2), pl.ds(g * HM, HM)], fr.at[it, g, src]
                    )
                relay(k, q).start()

        def imagine(k):
            for q in range(2):
                relay(k, q).wait_recv()
            for q in range(2):
                make_images(it, source_at(k, q))

        def send_next(k):
            @pl.when(k + WINDOW < pairs(it))
            def _():
                for g in range(2):
                    send_pair(it, pair_at(it, k + WINDOW), g)

            if it == 0:
                load_coupling(k).start()

        arrive(0)
        send_next(0)
        apply_mean(0)
        apply_mean(1)

        @pl.loop(1, D2)
        def _(k):
            arrive(k)
            send_next(k)
            imagine(k - 1)
            apply_mean(2 * k)
            apply_mean(2 * k + 1)

        imagine(D2 - 1)

        @pl.loop(0, D2)
        def _(k):
            for q in range(2):
                relay(k, q).wait_send()

        sent_pairs(it)
        if it == 0:

            @pl.loop(0, D2)
            def _(k):
                load_coupling(k).wait()


        def results(i):
            return (
                remote(outq.at[it, i], inq.at[it, d], os_.at[it, 0, i], or_.at[it, 0, d], i, s),
                remote(outs.at[it, i], ins.at[it, d], os_.at[it, 1, i], or_.at[it, 1, d], i, s),
            )

        def mix(i):
            count = count_s[i]
            lefts = []
            rights = []
            for k in range(MAXC):
                entry = jnp.where(k < count, list_s[k, i], 3 * D)
                lefts.append(coup_v[i, k])
                rights.append(images[entry])
            both = jnp.dot(
                jnp.concatenate(lefts, 1),
                jnp.concatenate(rights, 0),
                preferred_element_type=F32,
            )
            value = both[:, :cols] + both[:, cols:]
            peak = jnp.max(jnp.abs(value), axis=0, keepdims=True)
            peak = jnp.maximum(peak, 1e-30)
            outq[it, i] = jnp.round(value * (STEPS / peak)).astype(jnp.int16)
            outs[it, i] = peak * (1.0 / STEPS)

        @pl.loop(1, D2)
        def _(k):
            i = 2 * ((C + k) % D2)
            mix(i)
            mix(i + 1)
            for q in range(2):
                for copy in results(i + q):
                    copy.start()

        mix(2 * C)
        mix(2 * C + 1)
        for copy in results(partner):
            copy.start()
        pltpu.make_async_copy(outq.at[it, d], inq.at[it, d], or_.at[it, 0, d]).start()
        pltpu.make_async_copy(outs.at[it, d], ins.at[it, d], or_.at[it, 1, d]).start()

        if not last:
            low[...] = jnp.zeros((N, cols), F32)

        @pl.loop(0, D2)
        def _(k):
            a = 2 * ((C + 2 * D2 - 1 - k) % D2)
            for q in range(2):
                landed(inq.at[it, a + q], or_.at[it, 0, a + q])
                landed(ins.at[it, a + q], or_.at[it, 1, a + q])
            parts = []
            for q in range(2):
                x = a + q
                plane = r0[x] - inq[it, x].astype(F32) * ins[it, x]
                if last:
                    stage_b[pl.ds(x, N, stride=R), :] = plane
                    rh[x + 1] = transform(plane, fore_v[:, pl.ds(0, 2 * cols)])[0]
                else:
                    rh[x + 1], part = transform(plane, fore_v[...])
                    parts.append(tiled(part) * waves_v[x + 1])
            if not last:
                low[...] += flat(parts[0] + parts[1])

        @pl.loop(1, D)
        def _(t):
            for copy in results((d + t) % D):
                copy.wait_send()

        if last:
            store_r = pltpu.make_async_copy(stage_b, res_h, lsem.at[2])
            store_r.start()

        def swap_low(t):
            mine = low_ex.at[s]
            return remote(mine, mine, zs.at[t], zr.at[s], d, (s + t) % NS)

        if not last:
            low_ex[s] = low[...].astype(BF16)

            @pl.loop(1, NS)
            def _(t):
                swap_low(t).start()

        def swap(t, g):
            mine = ex.at[it, g, s]
            return remote(mine, mine, xs.at[it, g, t], xr.at[it, g, s], d, (s + t) % NS)

        for g in range(2):

            @pl.loop(0, HM // CH)
            def _(c):
                m = pl.multiple_of(c * CH, CH)
                ms = pl.ds(g * HM + m, CH)
                run = jnp.zeros((CH // 8, 8, cols), F32)
                head = jnp.zeros((CH // 8, 8, cols), F32)
                for x in range(R):
                    value = tiled(rh[x + 1, ms, :])
                    head = head + sweep_v[1, x] * value
                    run = (run + value) * sweep_v[0, x]
                    rh[x + 1, ms, :] = flat(run)
                ex[it, g, s, 0, pl.ds(m, CH), :] = flat(head)
                ex[it, g, s, 1, pl.ds(m, CH), :] = flat(run)

            @pl.loop(1, NS)
            def _(t):
                swap(t, g).start()

        for g in range(2):

            @pl.loop(1, NS)
            def _(t):
                other = (s + t) % NS
                landed(ex.at[it, g, other], xr.at[it, g, other])

            @pl.loop(0, HM // CH)
            def _(c):
                m = pl.multiple_of(c * CH, CH)
                ms = pl.ds(g * HM + m, CH)
                ends = [tiled(ex[it, g, k % NS, k // NS, pl.ds(m, CH), :]) for k in range(2 * NS)]
                outer = []
                for side_of in range(2):
                    total = meet_v[side_of, 0] * ends[0]
                    for k in range(1, 2 * NS):
                        total = total + meet_v[side_of, k] * ends[k]
                    outer.append(total)
                rh[0, ms, :] = flat(outer[0])
                rh[R + 1, ms, :] = flat(outer[1])
                run = outer[1]
                for x in reversed(range(R)):
                    run = (
                        tiled(rh[x + 1, ms, :]) + sweep_v[2, x] * outer[0] + sweep_v[0, x] * run
                    )
                    rh[x + 1, ms, :] = flat(run)

            half = pl.ds(g * HM, HM)
            if last:

                @pl.loop(0, D2)
                def _(i):
                    for h in range(2):
                        x = 2 * i + h + 1
                        change = transform(rh[x, half, :], back_v[pl.ds(0, 2 * cols), :])[0]
                        whole = pl.ds(g * HM * R + x - 1, HM, stride=R)
                        stage_g[whole, :] = u[x, half, :] + change

                part = pl.ds(g * HM * R, HM * R)
                pltpu.make_async_copy(stage_g.at[part], sol_h.at[part], lsem.at[3 + g]).start()

            else:
                if g == 0:

                    @pl.loop(1, NS)
                    def _(t):
                        other = (s + t) % NS
                        landed(low_ex.at[other], zr.at[other])

                    total = low_ex[0].astype(F32)
                    for k in range(1, NS):
                        total = total + low_ex[k].astype(F32)
                    low[...] = flat(tiled(total) * gap_v[...])

                @pl.loop(0, D2 + 1)
                def _(k):
                    i = (C + k) % (D2 + 1)
                    for h in range(2):
                        x = 2 * i + h
                        wave = flat(tiled(low[half, :]) * waves_v[x]).astype(BF16)
                        plane = u[x, half, :] + transform(rh[x, half, :], back_v[...], wave)[0]
                        u[x, half, :] = plane
                        sb[x, half, :] = plane.astype(BF16)

                    @pl.when(k < WINDOW)
                    def _():
                        send_pair(it + 1, i, g)

        @pl.loop(1, NS)
        def _(t):
            for g in range(2):
                swap(t, g).wait_send()
            if not last:
                swap_low(t).wait_send()

    store_r.wait()
    for g in range(2):
        part = pl.ds(g * HM * R, HM * R)
        pltpu.make_async_copy(stage_g.at[part], sol_h.at[part], lsem.at[3 + g]).wait()


def local(D, NS, interpret, guess, right_side, mean_coef, field_coef, coupling, listed, count):
    modes, R, cols = guess.shape
    N = BLK
    sine, sweep, meet, waves, gap = tables(R, cols, NS)
    fore = fore_table(sine)
    back = back_table(RELAX * sine.astype(np.float64))
    flat_shape = jax.ShapeDtypeStruct((modes * R, cols), F32)
    hbm = pl.BlockSpec(memory_space=pl.ANY)
    vmem = pl.BlockSpec(memory_space=pltpu.VMEM)
    smem = pl.BlockSpec(memory_space=pltpu.SMEM)
    sems = pltpu.SemaphoreType.DMA
    sol, res = pl.pallas_call(
        functools.partial(body, D, NS, R),
        out_shape=(flat_shape, flat_shape),
        in_specs=[smem, smem, hbm, hbm, vmem, vmem, hbm] + [hbm] * 5 + [vmem],
        out_specs=(hbm, hbm),
        scratch_shapes=[
            pltpu.VMEM((modes * R, cols), F32),
            pltpu.VMEM((modes * R, cols), F32),
            pltpu.VMEM(fore.shape, BF16),
            pltpu.VMEM(back.shape, BF16),
            pltpu.VMEM(sweep.shape, F32),
            pltpu.VMEM(meet.shape[1:], F32),
            pltpu.VMEM(waves.shape[1:], F32),
            pltpu.VMEM((D, MAXC, N, N), BF16),
            pltpu.VMEM((R + 2, N, cols), F32),
            pltpu.VMEM((R + 2, N, cols), BF16),
            pltpu.VMEM((R, N, cols), F32),
            pltpu.VMEM((R + 2, N, cols), F32),
            pltpu.VMEM((ITERS, D, 4, N, cols), BF16),
            pltpu.VMEM((FIELDS * D + 1, N, 2 * cols), BF16),
            pltpu.VMEM((ITERS, D, N, cols), jnp.int16),
            pltpu.VMEM((ITERS, D, 1, cols), F32),
            pltpu.VMEM((ITERS, R, N, cols), jnp.int16),
            pltpu.VMEM((ITERS, R, 1, cols), F32),
            pltpu.VMEM((ITERS, 2, NS, 2, N // 2, cols), F32),
            pltpu.VMEM((N, cols), F32),
            pltpu.VMEM((NS, N, cols), BF16),
            pltpu.VMEM((2, 8, cols), F32),
            pltpu.VMEM((2, 8, cols), F32),
            pltpu.VMEM((FIELDS + 1, R + 16, cols), F32),
            pltpu.VMEM((5, R, 8, cols), F32),
            pltpu.VMEM((FIELDS, 5, 8, cols), F32),
            sems((5,)),
            sems((4,)),
            sems((4,)),
            sems((ITERS, 2, D)),
            sems((ITERS, 2, D)),
            sems((ITERS, D)),
            sems((ITERS, D)),
            sems((ITERS, 2, D)),
            sems((ITERS, 2, D)),
            sems((ITERS, 2, NS)),
            sems((ITERS, 2, NS)),
            sems((NS,)),
            sems((NS,)),
            sems((5,)),
            sems((D // 2,)),
        ],
        compiler_params=pltpu.CompilerParams(
            collective_id=0, has_side_effects=True, vmem_limit_bytes=67043328
        ),
        interpret=interpret,
    )(
        listed.T,
        count,
        guess.reshape(modes * R, cols),
        right_side.reshape(modes * R, cols),
        mean_coef,
        field_coef,
        coupling,
        *(jnp.asarray(table) for table in (fore, back, sweep, meet, waves, gap)),
    )
    return sol.reshape(guess.shape), res.reshape(guess.shape)


def solution(mesh, interpret=False):
    placed = (
        P("mode", "slab", None),
        P("mode", "slab", None),
        P("slab", None),
        P(None, "slab", None),
        P(),
        P(),
        P(),
    )
    return jax.shard_map(
        functools.partial(local, mesh.shape["mode"], mesh.shape["slab"], interpret),
        mesh=mesh,
        in_specs=placed,
        out_specs=(P("mode", "slab", None), P("mode", "slab", None)),
        check_vma=False,
    )
```

```python
import functools
import math

import jax
import jax.numpy as jnp
import numpy as np
from jax import lax
from jax.experimental import pallas as pl
from jax.experimental.pallas import tpu as pltpu
from jax.sharding import PartitionSpec as P

FIELDS = 3
MAXC = 16
BLK = 128
ITERS = 2
RELAX = 0.6
STEPS = 32760.0
F32 = jnp.float32
BF16 = jnp.bfloat16


LOW_ROWS = 8
LOW_COLS = 16


def halves(table):
    hi = np.asarray(table, np.float32).astype(BF16)
    lo = (np.asarray(table, np.float32) - hi.astype(np.float32)).astype(BF16)
    return hi, lo, np.zeros_like(hi)


def fore_table(sine):
    hi, lo, zero = halves(sine)
    low = np.tile(hi[:, :LOW_COLS], (1, LOW_ROWS))
    return np.concatenate(
        [np.concatenate([hi, lo, low], 1), np.concatenate([hi, zero, zero], 1)], 0
    )


def back_table(sine):
    hi, lo, zero = halves(sine)
    low = np.tile(hi[:LOW_COLS], (LOW_ROWS, 1))
    return np.concatenate(
        [
            np.concatenate([hi, lo], 1),
            np.concatenate([hi, zero], 1),
            np.concatenate([low, zero], 1),
        ],
        0,
    )


def single(length):
    f32 = np.float32
    counter = np.arange(length).astype(f32) + f32(1.0)
    angle = f32(math.pi) * counter[:, None] * counter[None] / f32(length + 1)
    sine = np.sin(angle.astype(np.float64)).astype(f32)
    sine = f32(math.sqrt(2.0 / (length + 1))) * sine
    turn = f32(math.pi) * counter / f32(length + 1)
    return sine, f32(2.0) * np.cos(turn.astype(np.float64)).astype(f32)


def tables(rows, cols, slabs):
    length = rows * slabs
    sine, along = single(cols)
    across = single(length)[1]
    diag = 4.0 - along.astype(np.float64)
    pivot = np.zeros((rows, cols))
    pivot[0] = 1.0 / diag
    for x in range(1, rows):
        pivot[x] = 1.0 / (diag - pivot[x - 1])
    reach = np.cumprod(pivot, axis=0)
    first = np.zeros((rows, cols))
    meet = np.zeros((slabs, 2, 2 * slabs, cols))
    eye = np.eye(rows)
    shift = np.eye(rows, k=1) + np.eye(rows, k=-1)
    for q in range(cols):
        column = np.linalg.solve(diag[q] * eye - shift, eye[0])
        first[:, q] = column
        near, far = column[0], column[-1]
        system = np.eye(2 * slabs)
        for s in range(slabs):
            if s > 0:
                system[s, slabs + s - 1] -= near
                system[slabs + s, slabs + s - 1] -= far
            if s < slabs - 1:
                system[s, s + 1] -= far
                system[slabs + s, s + 1] -= near
        inverse = np.linalg.inv(system)
        for s in range(slabs):
            if s > 0:
                meet[s, 0, :, q] = inverse[slabs + s - 1]
            if s < slabs - 1:
                meet[s, 1, :, q] = inverse[s + 1]
    p = np.arange(LOW_ROWS)
    rounded = (np.float32(4.0) - across[:LOW_ROWS, None]) - along[None, :LOW_COLS]
    smooth = diag[None, :LOW_COLS] - 2.0 * np.cos(np.pi * (p + 1.0) / (length + 1))[:, None]
    gap = 1.0 / rounded.astype(np.float64) - 1.0 / smooth
    gap = np.broadcast_to(gap.reshape(1, cols), (8, cols)).astype(np.float32)
    place = np.arange(slabs)[:, None] * rows + np.arange(rows + 2)[None]
    waves = np.sqrt(2.0 / (length + 1)) * np.sin(
        np.pi * place[:, :, None] * (p + 1.0) / (length + 1)
    )
    waves = np.repeat(waves, LOW_COLS, axis=2)
    waves = np.broadcast_to(waves[:, :, None], (slabs, rows + 2, 8, cols)).astype(np.float32)
    sweep = np.stack([pivot, first, reach])
    sweep = np.broadcast_to(sweep[:, :, None], (3, rows, 8, cols)).astype(np.float32)
    meet = np.broadcast_to(meet[:, :, :, None], (slabs, 2, 2 * slabs, 8, cols)).astype(np.float32)
    return sine, sweep, meet, waves, gap


def crossing(cols):
    half = cols // 2
    pick = np.zeros((16, 2 * cols), np.float32)
    place = np.zeros((2, 16, cols), np.float32)
    for row in range(2):
        pick[2 * row, row * cols + half - 1] = 1.0
        pick[2 * row + 1, row * cols + half] = 1.0
        place[0, 2 * row + 1, row * half + half - 1] = 1.0
        place[1, 2 * row, row * half] = 1.0
    return pick.astype(BF16), place.astype(BF16)


def tiled(plane):
    return plane.reshape(plane.shape[0] // 8, 8, plane.shape[1])


def flat(plane):
    return plane.reshape(plane.shape[0] * 8, plane.shape[2])


def transform(plane, table, extra=None):
    hi = plane.astype(BF16)
    lo = (plane - hi.astype(F32)).astype(BF16)
    parts = [hi, lo] if extra is None else [hi, lo, extra]
    both = jnp.dot(jnp.concatenate(parts, 1), table, preferred_element_type=F32)
    cols = plane.shape[1]
    return both[:, :cols] + both[:, cols : 2 * cols], both[:, 2 * cols :]


def averages(center, above, below):
    cols = center.shape[1]
    lane = lax.broadcasted_iota(jnp.int32, center.shape, 1)
    left = 0.5 * (center + pltpu.roll(center, 1, 1))
    right = 0.5 * (center + pltpu.roll(center, cols - 1, 1))
    up = 0.5 * (center + above)
    down = 0.5 * (center + below)
    zero = jnp.zeros_like(center)
    total = (
        up + down + jnp.where(lane == 0, center, left) + jnp.where(lane == cols - 1, center, right)
    )
    return (
        total,
        jnp.where(lane == 0, zero, left),
        jnp.where(lane == cols - 1, zero, right),
        up,
        down,
    )


def body(
    D,
    NS,
    R,
    list_s,
    count_s,
    guess_h,
    right_h,
    mean_v,
    field_v,
    coup_h,
    fore_h,
    back_h,
    sweep_h,
    meet_h,
    waves_h,
    gap_v,
    pick_v,
    place_v,
    sol_h,
    res_h,
    stage_g,
    stage_b,
    fore_v,
    back_v,
    sweep_v,
    meet_v,
    waves_v,
    coup_v,
    u,
    packed,
    cross,
    cross_in,
    r0,
    rh,
    strips,
    images,
    outq,
    outs,
    inq,
    ins,
    ex,
    low,
    low_ex,
    edge,
    edge_in,
    cpad,
    mco,
    fco,
    lsem,
    hs,
    hr,
    fs,
    fr,
    ps,
    pr,
    os_,
    or_,
    xs,
    xr,
    zs,
    zr,
    table_sem,
    coup_sem,
):
    D2 = D // 2
    N = BLK
    cols = guess_h.shape[1]
    H = cols // 2
    lane = lax.broadcasted_iota(jnp.int32, (8, cols), 1)
    lane1 = lane[:1]
    d = lax.axis_index("mode")
    s = lax.axis_index("slab")
    C = d // 2
    p = d % 2
    partner = 2 * C + 1 - p
    above = (s + NS - 1) % NS
    below = (s + 1) % NS
    CH = 32

    def remote(src, dst, send, recv, mode, slab):
        return pltpu.make_async_remote_copy(
            src_ref=src,
            dst_ref=dst,
            send_sem=send,
            recv_sem=recv,
            device_id=(mode, slab),
            device_id_type=pl.DeviceIdType.MESH,
        )

    def landed(ref, sem):
        pltpu.make_async_copy(ref, ref, sem).wait()

    HM = N // 2
    load_g = pltpu.make_async_copy(guess_h, stage_g, lsem.at[0])
    load_b = pltpu.make_async_copy(right_h, stage_b, lsem.at[1])
    load_g.start()

    def load_coupling(k):
        some = pl.ds(2 * k, 2)
        return pltpu.make_async_copy(coup_h.at[some], coup_v.at[some], coup_sem.at[k])

    table_loads = [
        pltpu.make_async_copy(source, target, table_sem.at[n])
        for n, (source, target) in enumerate(
            (
                (fore_h, fore_v),
                (back_h, back_v),
                (sweep_h, sweep_v),
                (meet_h.at[s], meet_v),
                (waves_h.at[s], waves_v),
            )
        )
    ]

    barrier = pltpu.get_barrier_semaphore()

    @pl.loop(1, D)
    def _(t):
        pl.semaphore_signal(
            barrier, inc=1, device_id=((d + t) % D, s), device_id_type=pl.DeviceIdType.MESH
        )

    @pl.loop(1, NS)
    def _(t):
        pl.semaphore_signal(
            barrier, inc=1, device_id=(d, (s + t) % NS), device_id_type=pl.DeviceIdType.MESH
        )

    for f in range(FIELDS + 1):
        whole = mean_v[...] if f == 0 else field_v[f - 1]
        cpad[f, pl.ds(8, R), :] = whole
        edge[0, pl.ds(f, 1), :] = whole[:1]
        edge[1, pl.ds(f, 1), :] = whole[R - 1 :]
    images[3 * D] = jnp.zeros((N, 2 * cols), BF16)
    load_g.wait()

    def take(x):
        plane = stage_g[pl.ds(x, N, stride=R), :]
        u[x + 1] = plane

    take(0)
    take(R - 1)
    pl.semaphore_wait(barrier, D - 1 + NS - 1)

    halo_up = remote(u.at[1], u.at[R + 1], hs.at[0], hr.at[0], d, above)
    halo_down = remote(u.at[R], u.at[0], hs.at[1], hr.at[1], d, below)
    coef_up = remote(edge.at[0], edge_in.at[1], hs.at[2], hr.at[2], d, above)
    coef_down = remote(edge.at[1], edge_in.at[0], hs.at[3], hr.at[3], d, below)
    halo_up.start()
    halo_down.start()
    coef_up.start()
    coef_down.start()

    def blend(first, second):
        keep = lax.broadcasted_iota(jnp.int32, first.shape, 1) < H
        return (
            jnp.where(keep, first, pltpu.roll(second, H, 1)),
            jnp.where(keep, pltpu.roll(first, H, 1), second),
        )

    def tile_copies(it, c, h, g):
        j = 2 * c + h
        half = pl.ds(g * HM, HM)
        yield packed.at[c, h, :, half], strips.at[it, d, :, half], fs.at[it, g, j], fr.at[it, g, d]
        if g == 1:
            yield cross.at[c], cross_in.at[it, d], ps.at[it, j], pr.at[it, d]

    def send_tiles(it, c, g):
        half = pl.ds(g * HM, HM)
        rows4 = [u[2 * c + n, half, :] for n in range(4)]
        for n, (one, two) in enumerate(((1, 2), (0, 3))):
            for h, plane in enumerate(blend(rows4[one], rows4[two])):
                packed[c, h, n, half, :] = plane.astype(BF16)
        if g == 1:
            both = jnp.concatenate([u[2 * c + 1], u[2 * c + 2]], 1).astype(BF16)
            cross[c] = lax.dot_general(
                pick_v[...], both, (((1,), (1,)), ((), ())), preferred_element_type=F32
            ).astype(BF16)
        for h in range(2):
            j = 2 * c + h

            @pl.when(j != d)
            def _():
                for source, target, send, recv in tile_copies(it, c, h, g):
                    remote(source, target, send, recv, j, s).start()

            @pl.when(j == d)
            def _():
                for source, target, send, recv in tile_copies(it, c, h, g):
                    pltpu.make_async_copy(source, target, recv).start()

    def sent_tiles(it):
        @pl.loop(1, D)
        def _(t):
            j = (d + t) % D
            for g in range(2):
                for source, target, send, recv in tile_copies(it, j // 2, j % 2, g):
                    remote(source, target, send, recv, j, s).wait_send()

    @pl.loop(0, D2)
    def _(k):
        x = 2 * ((C + k) % D2)
        for h in range(2):

            @pl.when(jnp.logical_and(x + h != 0, x + h != R - 1))
            def _():
                take(x + h)

    @pl.loop(0, D2)
    def _(k):
        c = (C + k) % D2

        @pl.when(jnp.logical_and(c != 0, c != D2 - 1))
        def _():
            for g in range(2):
                send_tiles(0, c, g)

    load_b.start()
    for copy in table_loads:
        copy.start()

    coef_up.wait()
    coef_down.wait()
    for f in range(FIELDS + 1):
        whole = cpad[f, pl.ds(8, R), :]
        cpad[f, pl.ds(7, 1), :] = jnp.where(s == 0, whole[:1], edge_in[0, pl.ds(f, 1), :])
        cpad[f, pl.ds(8 + R, 1), :] = jnp.where(
            s == NS - 1, whole[R - 1 :], edge_in[1, pl.ds(f, 1), :]
        )
    halo_up.wait()
    halo_down.wait()
    top = jnp.where(s == 0, jnp.zeros((N, cols), F32), u[0])
    bottom = jnp.where(s == NS - 1, jnp.zeros((N, cols), F32), u[R + 1])
    u[0] = top
    u[R + 1] = bottom
    for c in (0, D2 - 1):
        for g in range(2):
            send_tiles(0, c, g)

    for n, value in enumerate(
        averages(cpad[0, pl.ds(8, R), :], cpad[0, pl.ds(7, R), :], cpad[0, pl.ds(9, R), :])
    ):
        mco[n] = jnp.broadcast_to(value[:, None, :], (R, 8, cols))
    for f in range(FIELDS):
        near = [cpad[f + 1, pl.ds(7 + 2 * C + n, 1), :] for n in range(4)]
        rows2 = [averages(near[n + 1], near[n], near[n + 2]) for n in range(2)]
        total, left, right, up, down = (
            jnp.where(p == 0, *blend(one, two)) for one, two in zip(*rows2)
        )
        zero = jnp.zeros_like(total)
        at_left = lane1 % H == 0
        at_right = lane1 % H == H - 1
        over = jnp.where(
            p == 0, jnp.where(at_right, right, zero), jnp.where(at_left, left, zero)
        )
        values = (
            total,
            jnp.where(at_left, zero, left),
            jnp.where(at_right, zero, right),
            jnp.where(lane1 < H, up, down),
            jnp.where(lane1 < H, down, up),
            over,
        )
        for n, value in enumerate(values):
            fco[f, n] = jnp.broadcast_to(value, (8, cols))
    load_b.wait()
    for copy in table_loads:
        copy.wait()

    def apply_mean(x):
        co = [mco[n, x] for n in range(5)]
        for m in range(0, N, CH):
            mid = u[x + 1, pl.ds(m, CH), :]
            left = pltpu.roll(mid, 1, 1)
            right = pltpu.roll(mid, cols - 1, 1)
            total = co[0] * tiled(mid) - co[1] * tiled(left) - co[2] * tiled(right)
            total = total - co[3] * tiled(u[x, pl.ds(m, CH), :])
            total = total - co[4] * tiled(u[x + 2, pl.ds(m, CH), :])
            side = stage_b[pl.ds(m * R + x, CH, stride=R), :]
            r0[x, pl.ds(m, CH), :] = side - flat(total)

    def make_images(it, src):
        edges = lax.dot_general(
            cross_in[it, src], place_v[p], (((0,), (0,)), ((), ())), preferred_element_type=F32
        )
        for m in range(0, N, CH):
            mid, far = (strips[it, src, n, pl.ds(m, CH), :].astype(F32) for n in range(2))
            terms = [
                tiled(term)
                for term in (
                    mid,
                    pltpu.roll(mid, 1, 1),
                    pltpu.roll(mid, cols - 1, 1),
                    far,
                    pltpu.roll(mid, H, 1),
                    edges[m : m + CH],
                )
            ]
            for f in range(FIELDS):
                value = fco[f, 0] * terms[0]
                for n in range(1, 6):
                    value = value - fco[f, n] * terms[n]
                value = flat(value)
                hi = value.astype(BF16)
                lo = (value - hi.astype(F32)).astype(BF16)
                images[3 * src + f, pl.ds(m, CH), :cols] = hi
                images[3 * src + f, pl.ds(m, CH), cols:] = lo

    for it in range(ITERS):
        last = it == ITERS - 1

        def source_at(k, q):
            return 2 * ((C + D2 - k) % D2) + q

        def arrive(k):
            for q in range(2):
                src = source_at(k, q)
                for g in range(2):
                    landed(strips.at[it, src, :, pl.ds(g * HM, HM)], fr.at[it, g, src])
                landed(cross_in.at[it, src], pr.at[it, src])

        @pl.loop(0, D2)
        def _(k):
            apply_mean(2 * k)
            apply_mean(2 * k + 1)

        @pl.loop(0, D2)
        def _(k):
            if it == 0:
                load_coupling(k).start()
            arrive(k)
            for q in range(2):
                make_images(it, source_at(k, q))

        sent_tiles(it)
        if it == 0:

            @pl.loop(0, D2)
            def _(k):
                load_coupling(k).wait()


        def results(i):
            return (
                remote(outq.at[it, i], inq.at[it, d], os_.at[it, 0, i], or_.at[it, 0, d], i, s),
                remote(outs.at[it, i], ins.at[it, d], os_.at[it, 1, i], or_.at[it, 1, d], i, s),
            )

        def mix(i):
            count = count_s[i]
            lefts = []
            rights = []
            for k in range(MAXC):
                entry = jnp.where(k < count, list_s[k, i], 3 * D)
                lefts.append(coup_v[i, k])
                rights.append(images[entry])
            both = jnp.dot(
                jnp.concatenate(lefts, 1),
                jnp.concatenate(rights, 0),
                preferred_element_type=F32,
            )
            value = both[:, :cols] + both[:, cols:]
            peak = jnp.max(jnp.abs(value), axis=0, keepdims=True)
            peak = jnp.maximum(peak, 1e-30)
            outq[it, i] = jnp.round(value * (STEPS / peak)).astype(jnp.int16)
            outs[it, i] = peak * (1.0 / STEPS)

        @pl.loop(1, D2)
        def _(k):
            i = 2 * ((C + k) % D2)
            mix(i)
            mix(i + 1)
            for q in range(2):
                for copy in results(i + q):
                    copy.start()

        mix(2 * C)
        mix(2 * C + 1)
        for copy in results(partner):
            copy.start()
        pltpu.make_async_copy(outq.at[it, d], inq.at[it, d], or_.at[it, 0, d]).start()
        pltpu.make_async_copy(outs.at[it, d], ins.at[it, d], or_.at[it, 1, d]).start()

        if not last:
            low[...] = jnp.zeros((N, cols), F32)

        @pl.loop(0, D2)
        def _(k):
            a = 2 * ((C + 2 * D2 - 1 - k) % D2)
            for q in range(2):
                landed(inq.at[it, a + q], or_.at[it, 0, a + q])
                landed(ins.at[it, a + q], or_.at[it, 1, a + q])
            parts = []
            terms = blend(*(inq[it, a + q].astype(F32) * ins[it, a + q] for q in range(2)))
            for q in range(2):
                x = a + q
                plane = r0[x] - terms[q]
                if last:
                    stage_b[pl.ds(x, N, stride=R), :] = plane
                    rh[x + 1] = transform(plane, fore_v[:, pl.ds(0, 2 * cols)])[0]
                else:
                    rh[x + 1], part = transform(plane, fore_v[...])
                    parts.append(tiled(part) * waves_v[x + 1])
            if not last:
                low[...] += flat(parts[0] + parts[1])

        @pl.loop(1, D)
        def _(t):
            for copy in results((d + t) % D):
                copy.wait_send()

        if last:
            store_r = pltpu.make_async_copy(stage_b, res_h, lsem.at[2])
            store_r.start()

        def swap_low(t):
            mine = low_ex.at[s]
            return remote(mine, mine, zs.at[t], zr.at[s], d, (s + t) % NS)

        if not last:
            low_ex[s] = low[...].astype(BF16)

            @pl.loop(1, NS)
            def _(t):
                swap_low(t).start()

        def swap(t, g):
            mine = ex.at[it, g, s]
            return remote(mine, mine, xs.at[it, g, t], xr.at[it, g, s], d, (s + t) % NS)

        for g in range(2):

            @pl.loop(0, HM // CH)
            def _(c):
                m = pl.multiple_of(c * CH, CH)
                ms = pl.ds(g * HM + m, CH)
                run = jnp.zeros((CH // 8, 8, cols), F32)
                head = jnp.zeros((CH // 8, 8, cols), F32)
                for x in range(R):
                    value = tiled(rh[x + 1, ms, :])
                    head = head + sweep_v[1, x] * value
                    run = (run + value) * sweep_v[0, x]
                    rh[x + 1, ms, :] = flat(run)
                ex[it, g, s, 0, pl.ds(m, CH), :] = flat(head)
                ex[it, g, s, 1, pl.ds(m, CH), :] = flat(run)

            @pl.loop(1, NS)
            def _(t):
                swap(t, g).start()

        for g in range(2):

            @pl.loop(1, NS)
            def _(t):
                other = (s + t) % NS
                landed(ex.at[it, g, other], xr.at[it, g, other])

            @pl.loop(0, HM // CH)
            def _(c):
                m = pl.multiple_of(c * CH, CH)
                ms = pl.ds(g * HM + m, CH)
                ends = [tiled(ex[it, g, k % NS, k // NS, pl.ds(m, CH), :]) for k in range(2 * NS)]
                outer = []
                for side_of in range(2):
                    total = meet_v[side_of, 0] * ends[0]
                    for k in range(1, 2 * NS):
                        total = total + meet_v[side_of, k] * ends[k]
                    outer.append(total)
                rh[0, ms, :] = flat(outer[0])
                rh[R + 1, ms, :] = flat(outer[1])
                run = outer[1]
                for x in reversed(range(R)):
                    run = (
                        tiled(rh[x + 1, ms, :]) + sweep_v[2, x] * outer[0] + sweep_v[0, x] * run
                    )
                    rh[x + 1, ms, :] = flat(run)

            half = pl.ds(g * HM, HM)
            if last:

                @pl.loop(0, D2)
                def _(i):
                    for h in range(2):
                        x = 2 * i + h + 1
                        change = transform(rh[x, half, :], back_v[pl.ds(0, 2 * cols), :])[0]
                        whole = pl.ds(g * HM * R + x - 1, HM, stride=R)
                        stage_g[whole, :] = u[x, half, :] + change

                part = pl.ds(g * HM * R, HM * R)
                pltpu.make_async_copy(stage_g.at[part], sol_h.at[part], lsem.at[3 + g]).start()

            else:
                if g == 0:

                    @pl.loop(1, NS)
                    def _(t):
                        other = (s + t) % NS
                        landed(low_ex.at[other], zr.at[other])

                    total = low_ex[0].astype(F32)
                    for k in range(1, NS):
                        total = total + low_ex[k].astype(F32)
                    low[...] = flat(tiled(total) * gap_v[...])

                @pl.loop(0, D2 + 1)
                def _(k):
                    i = (C + k) % (D2 + 1)
                    for h in range(2):
                        x = 2 * i + h
                        wave = flat(tiled(low[half, :]) * waves_v[x]).astype(BF16)
                        change = transform(rh[x, half, :], back_v[...], wave)[0]
                        u[x, half, :] = u[x, half, :] + change

                @pl.loop(0, D2)
                def _(k):
                    send_tiles(it + 1, (C + k) % D2, g)

        @pl.loop(1, NS)
        def _(t):
            for g in range(2):
                swap(t, g).wait_send()
            if not last:
                swap_low(t).wait_send()

    store_r.wait()
    for g in range(2):
        part = pl.ds(g * HM * R, HM * R)
        pltpu.make_async_copy(stage_g.at[part], sol_h.at[part], lsem.at[3 + g]).wait()


def local(D, NS, interpret, guess, right_side, mean_coef, field_coef, coupling, listed, count):
    modes, R, cols = guess.shape
    N = BLK
    sine, sweep, meet, waves, gap = tables(R, cols, NS)
    fore = fore_table(sine)
    back = back_table(RELAX * sine.astype(np.float64))
    flat_shape = jax.ShapeDtypeStruct((modes * R, cols), F32)
    hbm = pl.BlockSpec(memory_space=pl.ANY)
    vmem = pl.BlockSpec(memory_space=pltpu.VMEM)
    smem = pl.BlockSpec(memory_space=pltpu.SMEM)
    sems = pltpu.SemaphoreType.DMA
    sol, res = pl.pallas_call(
        functools.partial(body, D, NS, R),
        out_shape=(flat_shape, flat_shape),
        in_specs=[smem, smem, hbm, hbm, vmem, vmem, hbm] + [hbm] * 5 + [vmem] * 3,
        out_specs=(hbm, hbm),
        scratch_shapes=[
            pltpu.VMEM((modes * R, cols), F32),
            pltpu.VMEM((modes * R, cols), F32),
            pltpu.VMEM(fore.shape, BF16),
            pltpu.VMEM(back.shape, BF16),
            pltpu.VMEM(sweep.shape, F32),
            pltpu.VMEM(meet.shape[1:], F32),
            pltpu.VMEM(waves.shape[1:], F32),
            pltpu.VMEM((D, MAXC, N, N), BF16),
            pltpu.VMEM((R + 2, N, cols), F32),
            pltpu.VMEM((D // 2, 2, 2, N, cols), BF16),
            pltpu.VMEM((D // 2, 16, N), BF16),
            pltpu.VMEM((ITERS, D, 16, N), BF16),
            pltpu.VMEM((R, N, cols), F32),
            pltpu.VMEM((R + 2, N, cols), F32),
            pltpu.VMEM((ITERS, D, 2, N, cols), BF16),
            pltpu.VMEM((FIELDS * D + 1, N, 2 * cols), BF16),
            pltpu.VMEM((ITERS, D, N, cols), jnp.int16),
            pltpu.VMEM((ITERS, D, 1, cols), F32),
            pltpu.VMEM((ITERS, R, N, cols), jnp.int16),
            pltpu.VMEM((ITERS, R, 1, cols), F32),
            pltpu.VMEM((ITERS, 2, NS, 2, N // 2, cols), F32),
            pltpu.VMEM((N, cols), F32),
            pltpu.VMEM((NS, N, cols), BF16),
            pltpu.VMEM((2, 8, cols), F32),
            pltpu.VMEM((2, 8, cols), F32),
            pltpu.VMEM((FIELDS + 1, R + 16, cols), F32),
            pltpu.VMEM((5, R, 8, cols), F32),
            pltpu.VMEM((FIELDS, 6, 8, cols), F32),
            sems((5,)),
            sems((4,)),
            sems((4,)),
            sems((ITERS, 2, D)),
            sems((ITERS, 2, D)),
            sems((ITERS, D)),
            sems((ITERS, D)),
            sems((ITERS, 2, D)),
            sems((ITERS, 2, D)),
            sems((ITERS, 2, NS)),
            sems((ITERS, 2, NS)),
            sems((NS,)),
            sems((NS,)),
            sems((5,)),
            sems((D // 2,)),
        ],
        compiler_params=pltpu.CompilerParams(
            collective_id=0, has_side_effects=True, vmem_limit_bytes=67043328
        ),
        interpret=interpret,
    )(
        listed.T,
        count,
        guess.reshape(modes * R, cols),
        right_side.reshape(modes * R, cols),
        mean_coef,
        field_coef,
        coupling,
        *(jnp.asarray(table) for table in (fore, back, sweep, meet, waves, gap, *crossing(cols))),
    )
    return sol.reshape(guess.shape), res.reshape(guess.shape)


def solution(mesh, interpret=False):
    placed = (
        P("mode", "slab", None),
        P("mode", "slab", None),
        P("slab", None),
        P(None, "slab", None),
        P(),
        P(),
        P(),
    )
    return jax.shard_map(
        functools.partial(local, mesh.shape["mode"], mesh.shape["slab"], interpret),
        mesh=mesh,
        in_specs=placed,
        out_specs=(P("mode", "slab", None), P("mode", "slab", None)),
        check_vma=False,
    )
```

```python
import functools
import math

import jax
import jax.numpy as jnp
import numpy as np
from jax import lax
from jax.experimental import pallas as pl
from jax.experimental.pallas import tpu as pltpu
from jax.sharding import PartitionSpec as P

FIELDS = 3
MAXC = 16
BLK = 128
ITERS = 2
RELAX = 0.6
STEPS = 32760.0
F32 = jnp.float32
BF16 = jnp.bfloat16


LOW_ROWS = 8
LOW_COLS = 16


def halves(table):
    hi = np.asarray(table, np.float32).astype(BF16)
    lo = (np.asarray(table, np.float32) - hi.astype(np.float32)).astype(BF16)
    return hi, lo, np.zeros_like(hi)


def fore_table(sine):
    hi, lo, zero = halves(sine)
    low = np.tile(hi[:, :LOW_COLS], (1, LOW_ROWS))
    return np.concatenate(
        [np.concatenate([hi, lo, low], 1), np.concatenate([hi, zero, zero], 1)], 0
    )


def back_table(sine):
    hi, lo, zero = halves(sine)
    low = np.tile(hi[:LOW_COLS], (LOW_ROWS, 1))
    return np.concatenate(
        [
            np.concatenate([hi, lo], 1),
            np.concatenate([hi, zero], 1),
            np.concatenate([low, zero], 1),
        ],
        0,
    )


def single(length):
    f32 = np.float32
    counter = np.arange(length).astype(f32) + f32(1.0)
    angle = f32(math.pi) * counter[:, None] * counter[None] / f32(length + 1)
    sine = np.sin(angle.astype(np.float64)).astype(f32)
    sine = f32(math.sqrt(2.0 / (length + 1))) * sine
    turn = f32(math.pi) * counter / f32(length + 1)
    return sine, f32(2.0) * np.cos(turn.astype(np.float64)).astype(f32)


def tables(rows, cols, slabs):
    length = rows * slabs
    sine, along = single(cols)
    across = single(length)[1]
    diag = 4.0 - along.astype(np.float64)
    pivot = np.zeros((rows, cols))
    pivot[0] = 1.0 / diag
    for x in range(1, rows):
        pivot[x] = 1.0 / (diag - pivot[x - 1])
    reach = np.cumprod(pivot, axis=0)
    first = np.zeros((rows, cols))
    meet = np.zeros((slabs, 2, 2 * slabs, cols))
    eye = np.eye(rows)
    shift = np.eye(rows, k=1) + np.eye(rows, k=-1)
    for q in range(cols):
        column = np.linalg.solve(diag[q] * eye - shift, eye[0])
        first[:, q] = column
        near, far = column[0], column[-1]
        system = np.eye(2 * slabs)
        for s in range(slabs):
            if s > 0:
                system[s, slabs + s - 1] -= near
                system[slabs + s, slabs + s - 1] -= far
            if s < slabs - 1:
                system[s, s + 1] -= far
                system[slabs + s, s + 1] -= near
        inverse = np.linalg.inv(system)
        for s in range(slabs):
            if s > 0:
                meet[s, 0, :, q] = inverse[slabs + s - 1]
            if s < slabs - 1:
                meet[s, 1, :, q] = inverse[s + 1]
    p = np.arange(LOW_ROWS)
    rounded = (np.float32(4.0) - across[:LOW_ROWS, None]) - along[None, :LOW_COLS]
    smooth = diag[None, :LOW_COLS] - 2.0 * np.cos(np.pi * (p + 1.0) / (length + 1))[:, None]
    gap = 1.0 / rounded.astype(np.float64) - 1.0 / smooth
    gap = np.broadcast_to(gap.reshape(1, cols), (8, cols)).astype(np.float32)
    place = np.arange(slabs)[:, None] * rows + np.arange(rows + 2)[None]
    waves = np.sqrt(2.0 / (length + 1)) * np.sin(
        np.pi * place[:, :, None] * (p + 1.0) / (length + 1)
    )
    waves = np.repeat(waves, LOW_COLS, axis=2)
    waves = np.broadcast_to(waves[:, :, None], (slabs, rows + 2, 8, cols)).astype(np.float32)
    sweep = np.stack([pivot, first, reach])
    sweep = np.broadcast_to(sweep[:, :, None], (3, rows, 8, cols)).astype(np.float32)
    meet = np.broadcast_to(meet[:, :, :, None], (slabs, 2, 2 * slabs, 8, cols)).astype(np.float32)
    return sine, sweep, meet, waves, gap


def tiled(plane):
    return plane.reshape(plane.shape[0] // 8, 8, plane.shape[1])


def flat(plane):
    return plane.reshape(plane.shape[0] * 8, plane.shape[2])


def transform(plane, table, extra=None):
    hi = plane.astype(BF16)
    lo = (plane - hi.astype(F32)).astype(BF16)
    parts = [hi, lo] if extra is None else [hi, lo, extra]
    both = jnp.dot(jnp.concatenate(parts, 1), table, preferred_element_type=F32)
    cols = plane.shape[1]
    return both[:, :cols] + both[:, cols : 2 * cols], both[:, 2 * cols :]


def averages(center, above, below):
    cols = center.shape[1]
    lane = lax.broadcasted_iota(jnp.int32, center.shape, 1)
    left = 0.5 * (center + pltpu.roll(center, 1, 1))
    right = 0.5 * (center + pltpu.roll(center, cols - 1, 1))
    up = 0.5 * (center + above)
    down = 0.5 * (center + below)
    zero = jnp.zeros_like(center)
    total = (
        up + down + jnp.where(lane == 0, center, left) + jnp.where(lane == cols - 1, center, right)
    )
    return (
        total,
        jnp.where(lane == 0, zero, left),
        jnp.where(lane == cols - 1, zero, right),
        up,
        down,
    )


def body(
    D,
    NS,
    R,
    list_s,
    count_s,
    guess_h,
    right_h,
    mean_v,
    field_v,
    coup_h,
    fore_h,
    back_h,
    sweep_h,
    meet_h,
    waves_h,
    gap_v,
    sol_h,
    res_h,
    stage_g,
    stage_b,
    fore_v,
    back_v,
    sweep_v,
    meet_v,
    waves_v,
    coup_v,
    u,
    sb,
    r0,
    rh,
    strips,
    images,
    outq,
    outs,
    inq,
    ins,
    ex,
    low,
    low_ex,
    edge,
    edge_in,
    cpad,
    mco,
    fco,
    lsem,
    hs,
    hr,
    fs,
    fr,
    ps,
    pr,
    os_,
    or_,
    xs,
    xr,
    zs,
    zr,
    table_sem,
    coup_sem,
):
    D2 = D // 2
    N = BLK
    cols = guess_h.shape[1]
    d = lax.axis_index("mode")
    s = lax.axis_index("slab")
    C = d // 2
    p = d % 2
    partner = 2 * C + 1 - p
    above = (s + NS - 1) % NS
    below = (s + 1) % NS
    CH = 32

    def remote(src, dst, send, recv, mode, slab):
        return pltpu.make_async_remote_copy(
            src_ref=src,
            dst_ref=dst,
            send_sem=send,
            recv_sem=recv,
            device_id=(mode, slab),
            device_id_type=pl.DeviceIdType.MESH,
        )

    def landed(ref, sem):
        pltpu.make_async_copy(ref, ref, sem).wait()

    HM = N // 2
    load_g = pltpu.make_async_copy(guess_h, stage_g, lsem.at[0])
    load_b = pltpu.make_async_copy(right_h, stage_b, lsem.at[1])
    load_g.start()

    def load_coupling(k):
        some = pl.ds(2 * k, 2)
        return pltpu.make_async_copy(coup_h.at[some], coup_v.at[some], coup_sem.at[k])

    table_loads = [
        pltpu.make_async_copy(source, target, table_sem.at[n])
        for n, (source, target) in enumerate(
            (
                (fore_h, fore_v),
                (back_h, back_v),
                (sweep_h, sweep_v),
                (meet_h.at[s], meet_v),
                (waves_h.at[s], waves_v),
            )
        )
    ]

    barrier = pltpu.get_barrier_semaphore()

    @pl.loop(1, D)
    def _(t):
        pl.semaphore_signal(
            barrier, inc=1, device_id=((d + t) % D, s), device_id_type=pl.DeviceIdType.MESH
        )

    @pl.loop(1, NS)
    def _(t):
        pl.semaphore_signal(
            barrier, inc=1, device_id=(d, (s + t) % NS), device_id_type=pl.DeviceIdType.MESH
        )

    for f in range(FIELDS + 1):
        whole = mean_v[...] if f == 0 else field_v[f - 1]
        cpad[f, pl.ds(8, R), :] = whole
        edge[0, pl.ds(f, 1), :] = whole[:1]
        edge[1, pl.ds(f, 1), :] = whole[R - 1 :]
    images[3 * D] = jnp.zeros((N, 2 * cols), BF16)
    load_g.wait()

    def take(x):
        plane = stage_g[pl.ds(x, N, stride=R), :]
        u[x + 1] = plane
        sb[x + 1] = plane.astype(BF16)

    @pl.loop(0, D2)
    def _(k):
        take(2 * k)
        take(2 * k + 1)

    pl.semaphore_wait(barrier, D - 1 + NS - 1)

    halo_up = remote(u.at[1], u.at[R + 1], hs.at[0], hr.at[0], d, above)
    halo_down = remote(u.at[R], u.at[0], hs.at[1], hr.at[1], d, below)
    coef_up = remote(edge.at[0], edge_in.at[1], hs.at[2], hr.at[2], d, above)
    coef_down = remote(edge.at[1], edge_in.at[0], hs.at[3], hr.at[3], d, below)
    halo_up.start()
    halo_down.start()
    coef_up.start()
    coef_down.start()

    def pair_copies(it, i, g):
        source = sb.at[pl.ds(2 * i, 2), pl.ds(g * HM, HM)]
        for live, j, half in ((i < D2, 2 * i, 0), (i >= 1, 2 * i - 1, 1)):
            target = strips.at[it, d, pl.ds(2 * half, 2), pl.ds(g * HM, HM)]
            yield live, j, source, target

    def send_pair(it, i, g):
        for live, j, source, target in pair_copies(it, i, g):

            @pl.when(jnp.logical_and(live, j != d))
            def _():
                remote(source, target, fs.at[it, g, j], fr.at[it, g, d], j, s).start()

            @pl.when(jnp.logical_and(live, j == d))
            def _():
                pltpu.make_async_copy(source, target, fr.at[it, g, d]).start()

    def sent_pairs(it):
        @pl.loop(1, D)
        def _(t):
            j = (d + t) % D
            for g in range(2):
                source = sb.at[pl.ds(0, 2), pl.ds(g * HM, HM)]
                target = strips.at[it, d, pl.ds(0, 2), pl.ds(g * HM, HM)]
                remote(source, target, fs.at[it, g, j], fr.at[it, g, d], j, s).wait_send()

    @pl.loop(0, D2 - 1)
    def _(k):
        for g in range(2):
            send_pair(0, 1 + (C + D2 - 2 + k) % (D2 - 1), g)

    load_b.start()
    for copy in table_loads:
        copy.start()

    coef_up.wait()
    coef_down.wait()
    for f in range(FIELDS + 1):
        whole = cpad[f, pl.ds(8, R), :]
        cpad[f, pl.ds(7, 1), :] = jnp.where(s == 0, whole[:1], edge_in[0, pl.ds(f, 1), :])
        cpad[f, pl.ds(8 + R, 1), :] = jnp.where(
            s == NS - 1, whole[R - 1 :], edge_in[1, pl.ds(f, 1), :]
        )
    halo_up.wait()
    halo_down.wait()
    top = jnp.where(s == 0, jnp.zeros((N, cols), F32), u[0])
    bottom = jnp.where(s == NS - 1, jnp.zeros((N, cols), F32), u[R + 1])
    u[0] = top
    u[R + 1] = bottom
    sb[0] = top.astype(BF16)
    sb[R + 1] = bottom.astype(BF16)
    for g in range(2):
        send_pair(0, 0, g)
        send_pair(0, D2, g)

    for n, value in enumerate(
        averages(cpad[0, pl.ds(8, R), :], cpad[0, pl.ds(7, R), :], cpad[0, pl.ds(9, R), :])
    ):
        mco[n] = jnp.broadcast_to(value[:, None, :], (R, 8, cols))
    for f in range(FIELDS):
        rows3 = [
            jnp.broadcast_to(cpad[f + 1, pl.ds(7 + d + n, 1), :], (8, cols)) for n in range(3)
        ]
        for n, value in enumerate(averages(rows3[1], rows3[0], rows3[2])):
            fco[f, n] = value
    load_b.wait()
    for copy in table_loads:
        copy.wait()

    def apply_mean(x):
        co = [mco[n, x] for n in range(5)]
        for m in range(0, N, CH):
            mid = u[x + 1, pl.ds(m, CH), :]
            left = pltpu.roll(mid, 1, 1)
            right = pltpu.roll(mid, cols - 1, 1)
            total = co[0] * tiled(mid) - co[1] * tiled(left) - co[2] * tiled(right)
            total = total - co[3] * tiled(u[x, pl.ds(m, CH), :])
            total = total - co[4] * tiled(u[x + 2, pl.ds(m, CH), :])
            side = stage_b[pl.ds(m * R + x, CH, stride=R), :]
            r0[x, pl.ds(m, CH), :] = side - flat(total)

    def make_images(it, src):
        for m in range(0, N, CH):
            up, mid, down = (
                strips[it, src, p + n, pl.ds(m, CH), :].astype(F32) for n in range(3)
            )
            left = tiled(pltpu.roll(mid, 1, 1))
            right = tiled(pltpu.roll(mid, cols - 1, 1))
            up, mid, down = tiled(up), tiled(mid), tiled(down)
            for f in range(FIELDS):
                value = flat(
                    fco[f, 0] * mid
                    - fco[f, 1] * left
                    - fco[f, 2] * right
                    - fco[f, 3] * up
                    - fco[f, 4] * down
                )
                hi = value.astype(BF16)
                lo = (value - hi.astype(F32)).astype(BF16)
                images[3 * src + f, pl.ds(m, CH), :cols] = hi
                images[3 * src + f, pl.ds(m, CH), cols:] = lo

    for it in range(ITERS):
        last = it == ITERS - 1

        def source_at(k, q):
            return 2 * ((C + D2 - k) % D2) + q

        def relay(k, q):
            src = source_at(k, q)
            shared = strips.at[it, src, 1 + p]
            return remote(shared, shared, ps.at[it, src], pr.at[it, src], partner, s)

        def arrive(k):
            for q in range(2):
                src = source_at(k, q)
                for g in range(2):
                    landed(
                        strips.at[it, src, pl.ds(2 * p, 2), pl.ds(g * HM, HM)], fr.at[it, g, src]
                    )
                relay(k, q).start()

        def imagine(k):
            for q in range(2):
                relay(k, q).wait_recv()
            for q in range(2):
                make_images(it, source_at(k, q))

        @pl.loop(0, D2)
        def _(k):
            apply_mean(2 * k)
            apply_mean(2 * k + 1)

        def load_some(k):
            if it == 0:
                load_coupling(k).start()

        arrive(0)
        load_some(0)
        @pl.loop(1, D2)
        def _(k):
            arrive(k)
            load_some(k)
            imagine(k - 1)

        imagine(D2 - 1)

        @pl.loop(0, D2)
        def _(k):
            for q in range(2):
                relay(k, q).wait_send()

        sent_pairs(it)
        if it == 0:

            @pl.loop(0, D2)
            def _(k):
                load_coupling(k).wait()


        def results(i):
            return (
                remote(outq.at[it, i], inq.at[it, d], os_.at[it, 0, i], or_.at[it, 0, d], i, s),
                remote(outs.at[it, i], ins.at[it, d], os_.at[it, 1, i], or_.at[it, 1, d], i, s),
            )

        def mix(i):
            count = count_s[i]
            lefts = []
            rights = []
            for k in range(MAXC):
                entry = jnp.where(k < count, list_s[k, i], 3 * D)
                lefts.append(coup_v[i, k])
                rights.append(images[entry])
            both = jnp.dot(
                jnp.concatenate(lefts, 1),
                jnp.concatenate(rights, 0),
                preferred_element_type=F32,
            )
            value = both[:, :cols] + both[:, cols:]
            peak = jnp.max(jnp.abs(value), axis=0, keepdims=True)
            peak = jnp.maximum(peak, 1e-30)
            outq[it, i] = jnp.round(value * (STEPS / peak)).astype(jnp.int16)
            outs[it, i] = peak * (1.0 / STEPS)

        @pl.loop(1, D2)
        def _(k):
            i = 2 * ((C + k) % D2)
            mix(i)
            mix(i + 1)
            for q in range(2):
                for copy in results(i + q):
                    copy.start()

        mix(2 * C)
        mix(2 * C + 1)
        for copy in results(partner):
            copy.start()
        pltpu.make_async_copy(outq.at[it, d], inq.at[it, d], or_.at[it, 0, d]).start()
        pltpu.make_async_copy(outs.at[it, d], ins.at[it, d], or_.at[it, 1, d]).start()

        if not last:
            low[...] = jnp.zeros((N, cols), F32)

        @pl.loop(0, D2)
        def _(k):
            a = 2 * ((C + 2 * D2 - 1 - k) % D2)
            for q in range(2):
                landed(inq.at[it, a + q], or_.at[it, 0, a + q])
                landed(ins.at[it, a + q], or_.at[it, 1, a + q])
            parts = []
            for q in range(2):
                x = a + q
                plane = r0[x] - inq[it, x].astype(F32) * ins[it, x]
                if last:
                    stage_b[pl.ds(x, N, stride=R), :] = plane
                    rh[x + 1] = transform(plane, fore_v[:, pl.ds(0, 2 * cols)])[0]
                else:
                    rh[x + 1], part = transform(plane, fore_v[...])
                    parts.append(tiled(part) * waves_v[x + 1])
            if not last:
                low[...] += flat(parts[0] + parts[1])

        @pl.loop(1, D)
        def _(t):
            for copy in results((d + t) % D):
                copy.wait_send()

        if last:
            store_r = pltpu.make_async_copy(stage_b, res_h, lsem.at[2])
            store_r.start()

        def swap_low(t):
            mine = low_ex.at[s]
            return remote(mine, mine, zs.at[t], zr.at[s], d, (s + t) % NS)

        if not last:
            low_ex[s] = low[...].astype(BF16)

        def swap(t, g):
            mine = ex.at[it, g, s]
            return remote(mine, mine, xs.at[it, g, t], xr.at[it, g, s], d, (s + t) % NS)

        for g in range(2):

            @pl.loop(0, HM // CH)
            def _(c):
                m = pl.multiple_of(c * CH, CH)
                ms = pl.ds(g * HM + m, CH)
                run = jnp.zeros((CH // 8, 8, cols), F32)
                head = jnp.zeros((CH // 8, 8, cols), F32)
                for x in range(R):
                    value = tiled(rh[x + 1, ms, :])
                    head = head + sweep_v[1, x] * value
                    run = (run + value) * sweep_v[0, x]
                    rh[x + 1, ms, :] = flat(run)
                ex[it, g, s, 0, pl.ds(m, CH), :] = flat(head)
                ex[it, g, s, 1, pl.ds(m, CH), :] = flat(run)

            @pl.loop(1, NS)
            def _(t):
                swap(t, g).start()
                if g == 0 and not last:
                    swap_low(t).start()

        for g in range(2):

            @pl.loop(1, NS)
            def _(t):
                other = (s + t) % NS
                landed(ex.at[it, g, other], xr.at[it, g, other])

            @pl.loop(0, HM // CH)
            def _(c):
                m = pl.multiple_of(c * CH, CH)
                ms = pl.ds(g * HM + m, CH)
                ends = [tiled(ex[it, g, k % NS, k // NS, pl.ds(m, CH), :]) for k in range(2 * NS)]
                outer = []
                for side_of in range(2):
                    total = meet_v[side_of, 0] * ends[0]
                    for k in range(1, 2 * NS):
                        total = total + meet_v[side_of, k] * ends[k]
                    outer.append(total)
                rh[0, ms, :] = flat(outer[0])
                rh[R + 1, ms, :] = flat(outer[1])
                run = outer[1]
                for x in reversed(range(R)):
                    run = (
                        tiled(rh[x + 1, ms, :]) + sweep_v[2, x] * outer[0] + sweep_v[0, x] * run
                    )
                    rh[x + 1, ms, :] = flat(run)

            half = pl.ds(g * HM, HM)
            if last:

                @pl.loop(0, D2)
                def _(i):
                    for h in range(2):
                        x = 2 * i + h + 1
                        change = transform(rh[x, half, :], back_v[pl.ds(0, 2 * cols), :])[0]
                        whole = pl.ds(g * HM * R + x - 1, HM, stride=R)
                        stage_g[whole, :] = u[x, half, :] + change

                part = pl.ds(g * HM * R, HM * R)
                pltpu.make_async_copy(stage_g.at[part], sol_h.at[part], lsem.at[3 + g]).start()

            else:
                if g == 0:

                    @pl.loop(1, NS)
                    def _(t):
                        other = (s + t) % NS
                        landed(low_ex.at[other], zr.at[other])

                    total = low_ex[0].astype(F32)
                    for k in range(1, NS):
                        total = total + low_ex[k].astype(F32)
                    low[...] = flat(tiled(total) * gap_v[...])

                @pl.loop(0, D2 + 1)
                def _(k):
                    i = (C + k) % (D2 + 1)
                    for h in range(2):
                        x = 2 * i + h
                        wave = flat(tiled(low[half, :]) * waves_v[x]).astype(BF16)
                        plane = u[x, half, :] + transform(rh[x, half, :], back_v[...], wave)[0]
                        u[x, half, :] = plane
                        sb[x, half, :] = plane.astype(BF16)
                    send_pair(it + 1, i, g)

        @pl.loop(1, NS)
        def _(t):
            for g in range(2):
                swap(t, g).wait_send()
            if not last:
                swap_low(t).wait_send()

    store_r.wait()
    for g in range(2):
        part = pl.ds(g * HM * R, HM * R)
        pltpu.make_async_copy(stage_g.at[part], sol_h.at[part], lsem.at[3 + g]).wait()


def local(D, NS, interpret, guess, right_side, mean_coef, field_coef, coupling, listed, count):
    modes, R, cols = guess.shape
    N = BLK
    sine, sweep, meet, waves, gap = tables(R, cols, NS)
    fore = fore_table(sine)
    back = back_table(RELAX * sine.astype(np.float64))
    flat_shape = jax.ShapeDtypeStruct((modes * R, cols), F32)
    hbm = pl.BlockSpec(memory_space=pl.ANY)
    vmem = pl.BlockSpec(memory_space=pltpu.VMEM)
    smem = pl.BlockSpec(memory_space=pltpu.SMEM)
    sems = pltpu.SemaphoreType.DMA
    sol, res = pl.pallas_call(
        functools.partial(body, D, NS, R),
        out_shape=(flat_shape, flat_shape),
        in_specs=[smem, smem, hbm, hbm, vmem, vmem, hbm] + [hbm] * 5 + [vmem],
        out_specs=(hbm, hbm),
        scratch_shapes=[
            pltpu.VMEM((modes * R, cols), F32),
            pltpu.VMEM((modes * R, cols), F32),
            pltpu.VMEM(fore.shape, BF16),
            pltpu.VMEM(back.shape, BF16),
            pltpu.VMEM(sweep.shape, F32),
            pltpu.VMEM(meet.shape[1:], F32),
            pltpu.VMEM(waves.shape[1:], F32),
            pltpu.VMEM((D, MAXC, N, N), BF16),
            pltpu.VMEM((R + 2, N, cols), F32),
            pltpu.VMEM((R + 2, N, cols), BF16),
            pltpu.VMEM((R, N, cols), F32),
            pltpu.VMEM((R + 2, N, cols), F32),
            pltpu.VMEM((ITERS, D, 4, N, cols), BF16),
            pltpu.VMEM((FIELDS * D + 1, N, 2 * cols), BF16),
            pltpu.VMEM((ITERS, D, N, cols), jnp.int16),
            pltpu.VMEM((ITERS, D, 1, cols), F32),
            pltpu.VMEM((ITERS, R, N, cols), jnp.int16),
            pltpu.VMEM((ITERS, R, 1, cols), F32),
            pltpu.VMEM((ITERS, 2, NS, 2, N // 2, cols), F32),
            pltpu.VMEM((N, cols), F32),
            pltpu.VMEM((NS, N, cols), BF16),
            pltpu.VMEM((2, 8, cols), F32),
            pltpu.VMEM((2, 8, cols), F32),
            pltpu.VMEM((FIELDS + 1, R + 16, cols), F32),
            pltpu.VMEM((5, R, 8, cols), F32),
            pltpu.VMEM((FIELDS, 5, 8, cols), F32),
            sems((5,)),
            sems((4,)),
            sems((4,)),
            sems((ITERS, 2, D)),
            sems((ITERS, 2, D)),
            sems((ITERS, D)),
            sems((ITERS, D)),
            sems((ITERS, 2, D)),
            sems((ITERS, 2, D)),
            sems((ITERS, 2, NS)),
            sems((ITERS, 2, NS)),
            sems((NS,)),
            sems((NS,)),
            sems((5,)),
            sems((D // 2,)),
        ],
        compiler_params=pltpu.CompilerParams(
            collective_id=0, has_side_effects=True, vmem_limit_bytes=67043328
        ),
        interpret=interpret,
    )(
        listed.T,
        count,
        guess.reshape(modes * R, cols),
        right_side.reshape(modes * R, cols),
        mean_coef,
        field_coef,
        coupling,
        *(jnp.asarray(table) for table in (fore, back, sweep, meet, waves, gap)),
    )
    return sol.reshape(guess.shape), res.reshape(guess.shape)


def solution(mesh, interpret=False):
    placed = (
        P("mode", "slab", None),
        P("mode", "slab", None),
        P("slab", None),
        P(None, "slab", None),
        P(),
        P(),
        P(),
    )
    return jax.shard_map(
        functools.partial(local, mesh.shape["mode"], mesh.shape["slab"], interpret),
        mesh=mesh,
        in_specs=placed,
        out_specs=(P("mode", "slab", None), P("mode", "slab", None)),
        check_vma=False,
    )
```

```python
import functools
import math

import jax
import jax.numpy as jnp
import numpy as np
from jax import lax
from jax.experimental import pallas as pl
from jax.experimental.pallas import tpu as pltpu
from jax.sharding import PartitionSpec as P

FIELDS = 3
MAXC = 16
BLK = 128
ITERS = 2
RELAX = 0.6
STEPS = 32760.0
F32 = jnp.float32
BF16 = jnp.bfloat16


LOW_ROWS = 8
LOW_COLS = 16


def halves(table):
    hi = np.asarray(table, np.float32).astype(BF16)
    lo = (np.asarray(table, np.float32) - hi.astype(np.float32)).astype(BF16)
    return hi, lo, np.zeros_like(hi)


def fore_table(sine):
    hi, lo, zero = halves(sine)
    low = np.tile(hi[:, :LOW_COLS], (1, LOW_ROWS))
    return np.concatenate(
        [np.concatenate([hi, lo, low], 1), np.concatenate([hi, zero, zero], 1)], 0
    )


def back_table(sine):
    hi, lo, zero = halves(sine)
    low = np.tile(hi[:LOW_COLS], (LOW_ROWS, 1))
    return np.concatenate(
        [
            np.concatenate([hi, lo], 1),
            np.concatenate([hi, zero], 1),
            np.concatenate([low, zero], 1),
        ],
        0,
    )


def single(length):
    f32 = np.float32
    counter = np.arange(length).astype(f32) + f32(1.0)
    angle = f32(math.pi) * counter[:, None] * counter[None] / f32(length + 1)
    sine = np.sin(angle.astype(np.float64)).astype(f32)
    sine = f32(math.sqrt(2.0 / (length + 1))) * sine
    turn = f32(math.pi) * counter / f32(length + 1)
    return sine, f32(2.0) * np.cos(turn.astype(np.float64)).astype(f32)


def tables(rows, cols, slabs):
    length = rows * slabs
    sine, along = single(cols)
    across = single(length)[1]
    diag = 4.0 - along.astype(np.float64)
    pivot = np.zeros((rows, cols))
    pivot[0] = 1.0 / diag
    for x in range(1, rows):
        pivot[x] = 1.0 / (diag - pivot[x - 1])
    reach = np.cumprod(pivot, axis=0)
    first = np.zeros((rows, cols))
    meet = np.zeros((slabs, 2, 2 * slabs, cols))
    eye = np.eye(rows)
    shift = np.eye(rows, k=1) + np.eye(rows, k=-1)
    for q in range(cols):
        column = np.linalg.solve(diag[q] * eye - shift, eye[0])
        first[:, q] = column
        near, far = column[0], column[-1]
        system = np.eye(2 * slabs)
        for s in range(slabs):
            if s > 0:
                system[s, slabs + s - 1] -= near
                system[slabs + s, slabs + s - 1] -= far
            if s < slabs - 1:
                system[s, s + 1] -= far
                system[slabs + s, s + 1] -= near
        inverse = np.linalg.inv(system)
        for s in range(slabs):
            if s > 0:
                meet[s, 0, :, q] = inverse[slabs + s - 1]
            if s < slabs - 1:
                meet[s, 1, :, q] = inverse[s + 1]
    p = np.arange(LOW_ROWS)
    rounded = (np.float32(4.0) - across[:LOW_ROWS, None]) - along[None, :LOW_COLS]
    smooth = diag[None, :LOW_COLS] - 2.0 * np.cos(np.pi * (p + 1.0) / (length + 1))[:, None]
    gap = 1.0 / rounded.astype(np.float64) - 1.0 / smooth
    gap = np.broadcast_to(gap.reshape(1, cols), (8, cols)).astype(np.float32)
    place = np.arange(slabs)[:, None] * rows + np.arange(rows + 2)[None]
    waves = np.sqrt(2.0 / (length + 1)) * np.sin(
        np.pi * place[:, :, None] * (p + 1.0) / (length + 1)
    )
    waves = np.repeat(waves, LOW_COLS, axis=2)
    waves = np.broadcast_to(waves[:, :, None], (slabs, rows + 2, 8, cols)).astype(np.float32)
    sweep = np.stack([pivot, first, reach])
    sweep = np.broadcast_to(sweep[:, :, None], (3, rows, 8, cols)).astype(np.float32)
    meet = np.broadcast_to(meet[:, :, :, None], (slabs, 2, 2 * slabs, 8, cols)).astype(np.float32)
    return sine, sweep, meet, waves, gap


def tiled(plane):
    return plane.reshape(plane.shape[0] // 8, 8, plane.shape[1])


def flat(plane):
    return plane.reshape(plane.shape[0] * 8, plane.shape[2])


def transform(plane, table, extra=None):
    hi = plane.astype(BF16)
    lo = (plane - hi.astype(F32)).astype(BF16)
    parts = [hi, lo] if extra is None else [hi, lo, extra]
    both = jnp.dot(jnp.concatenate(parts, 1), table, preferred_element_type=F32)
    cols = plane.shape[1]
    return both[:, :cols] + both[:, cols : 2 * cols], both[:, 2 * cols :]


def averages(center, above, below):
    cols = center.shape[1]
    lane = lax.broadcasted_iota(jnp.int32, center.shape, 1)
    left = 0.5 * (center + pltpu.roll(center, 1, 1))
    right = 0.5 * (center + pltpu.roll(center, cols - 1, 1))
    up = 0.5 * (center + above)
    down = 0.5 * (center + below)
    zero = jnp.zeros_like(center)
    total = (
        up + down + jnp.where(lane == 0, center, left) + jnp.where(lane == cols - 1, center, right)
    )
    return (
        total,
        jnp.where(lane == 0, zero, left),
        jnp.where(lane == cols - 1, zero, right),
        up,
        down,
    )


def body(
    D,
    NS,
    R,
    list_s,
    count_s,
    guess_h,
    right_h,
    mean_v,
    field_v,
    coup_h,
    fore_h,
    back_h,
    sweep_h,
    meet_h,
    waves_h,
    gap_v,
    sol_h,
    res_h,
    stage_g,
    stage_b,
    fore_v,
    back_v,
    sweep_v,
    meet_v,
    waves_v,
    coup_v,
    u,
    sb,
    r0,
    rh,
    strips,
    images,
    outq,
    outs,
    inq,
    ins,
    ex,
    low,
    low_ex,
    edge,
    edge_in,
    cpad,
    mco,
    fco,
    lsem,
    hs,
    hr,
    fs,
    fr,
    ps,
    pr,
    os_,
    or_,
    xs,
    xr,
    zs,
    zr,
    table_sem,
    coup_sem,
):
    D2 = D // 2
    N = BLK
    cols = guess_h.shape[1]
    d = lax.axis_index("mode")
    s = lax.axis_index("slab")
    C = d // 2
    p = d % 2
    partner = 2 * C + 1 - p
    above = (s + NS - 1) % NS
    below = (s + 1) % NS
    CH = 32

    def remote(src, dst, send, recv, mode, slab):
        return pltpu.make_async_remote_copy(
            src_ref=src,
            dst_ref=dst,
            send_sem=send,
            recv_sem=recv,
            device_id=(mode, slab),
            device_id_type=pl.DeviceIdType.MESH,
        )

    def landed(ref, sem):
        pltpu.make_async_copy(ref, ref, sem).wait()

    HM = N // 2
    load_g = pltpu.make_async_copy(guess_h, stage_g, lsem.at[0])
    load_b = pltpu.make_async_copy(right_h, stage_b, lsem.at[1])
    load_g.start()

    def load_coupling(k):
        some = pl.ds(2 * k, 2)
        return pltpu.make_async_copy(coup_h.at[some], coup_v.at[some], coup_sem.at[k])

    table_loads = [
        pltpu.make_async_copy(source, target, table_sem.at[n])
        for n, (source, target) in enumerate(
            (
                (fore_h, fore_v),
                (back_h, back_v),
                (sweep_h, sweep_v),
                (meet_h.at[s], meet_v),
                (waves_h.at[s], waves_v),
            )
        )
    ]

    barrier = pltpu.get_barrier_semaphore()

    @pl.loop(1, D)
    def _(t):
        pl.semaphore_signal(
            barrier, inc=1, device_id=((d + t) % D, s), device_id_type=pl.DeviceIdType.MESH
        )

    @pl.loop(1, NS)
    def _(t):
        pl.semaphore_signal(
            barrier, inc=1, device_id=(d, (s + t) % NS), device_id_type=pl.DeviceIdType.MESH
        )

    for f in range(FIELDS + 1):
        whole = mean_v[...] if f == 0 else field_v[f - 1]
        cpad[f, pl.ds(8, R), :] = whole
        edge[0, pl.ds(f, 1), :] = whole[:1]
        edge[1, pl.ds(f, 1), :] = whole[R - 1 :]
    images[3 * D] = jnp.zeros((N, 2 * cols), BF16)
    load_g.wait()

    def take(x):
        plane = stage_g[pl.ds(x, N, stride=R), :]
        u[x + 1] = plane
        sb[x + 1] = plane.astype(BF16)

    @pl.loop(0, D2)
    def _(k):
        take(2 * k)
        take(2 * k + 1)

    pl.semaphore_wait(barrier, D - 1 + NS - 1)

    halo_up = remote(u.at[1], u.at[R + 1], hs.at[0], hr.at[0], d, above)
    halo_down = remote(u.at[R], u.at[0], hs.at[1], hr.at[1], d, below)
    coef_up = remote(edge.at[0], edge_in.at[1], hs.at[2], hr.at[2], d, above)
    coef_down = remote(edge.at[1], edge_in.at[0], hs.at[3], hr.at[3], d, below)
    halo_up.start()
    halo_down.start()
    coef_up.start()
    coef_down.start()

    def pair_copies(it, i, g):
        source = sb.at[pl.ds(2 * i, 2), pl.ds(g * HM, HM)]
        for live, j, half in ((i < D2, 2 * i, 0), (i >= 1, 2 * i - 1, 1)):
            target = strips.at[it, d, pl.ds(2 * half, 2), pl.ds(g * HM, HM)]
            yield live, j, source, target

    def send_pair(it, i, g):
        for live, j, source, target in pair_copies(it, i, g):

            @pl.when(jnp.logical_and(live, j != d))
            def _():
                remote(source, target, fs.at[it, g, j], fr.at[it, g, d], j, s).start()

            @pl.when(jnp.logical_and(live, j == d))
            def _():
                pltpu.make_async_copy(source, target, fr.at[it, g, d]).start()

    def sent_pairs(it):
        @pl.loop(1, D)
        def _(t):
            j = (d + t) % D
            for g in range(2):
                source = sb.at[pl.ds(0, 2), pl.ds(g * HM, HM)]
                target = strips.at[it, d, pl.ds(0, 2), pl.ds(g * HM, HM)]
                remote(source, target, fs.at[it, g, j], fr.at[it, g, d], j, s).wait_send()

    @pl.loop(0, D2 - 1)
    def _(k):
        for g in range(2):
            send_pair(0, 1 + (C + D2 - 2 + k) % (D2 - 1), g)

    load_b.start()
    for copy in table_loads:
        copy.start()

    coef_up.wait()
    coef_down.wait()
    for f in range(FIELDS + 1):
        whole = cpad[f, pl.ds(8, R), :]
        cpad[f, pl.ds(7, 1), :] = jnp.where(s == 0, whole[:1], edge_in[0, pl.ds(f, 1), :])
        cpad[f, pl.ds(8 + R, 1), :] = jnp.where(
            s == NS - 1, whole[R - 1 :], edge_in[1, pl.ds(f, 1), :]
        )
    halo_up.wait()
    halo_down.wait()
    top = jnp.where(s == 0, jnp.zeros((N, cols), F32), u[0])
    bottom = jnp.where(s == NS - 1, jnp.zeros((N, cols), F32), u[R + 1])
    u[0] = top
    u[R + 1] = bottom
    sb[0] = top.astype(BF16)
    sb[R + 1] = bottom.astype(BF16)
    for g in range(2):
        send_pair(0, 0, g)
        send_pair(0, D2, g)

    for n, value in enumerate(
        averages(cpad[0, pl.ds(8, R), :], cpad[0, pl.ds(7, R), :], cpad[0, pl.ds(9, R), :])
    ):
        mco[n] = jnp.broadcast_to(value[:, None, :], (R, 8, cols))
    for f in range(FIELDS):
        rows3 = [
            jnp.broadcast_to(cpad[f + 1, pl.ds(7 + d + n, 1), :], (8, cols)) for n in range(3)
        ]
        for n, value in enumerate(averages(rows3[1], rows3[0], rows3[2])):
            fco[f, n] = value
    load_b.wait()
    for copy in table_loads:
        copy.wait()

    def apply_mean(x):
        co = [mco[n, x] for n in range(5)]
        for m in range(0, N, CH):
            mid = u[x + 1, pl.ds(m, CH), :]
            left = pltpu.roll(mid, 1, 1)
            right = pltpu.roll(mid, cols - 1, 1)
            total = co[0] * tiled(mid) - co[1] * tiled(left) - co[2] * tiled(right)
            total = total - co[3] * tiled(u[x, pl.ds(m, CH), :])
            total = total - co[4] * tiled(u[x + 2, pl.ds(m, CH), :])
            side = stage_b[pl.ds(m * R + x, CH, stride=R), :]
            r0[x, pl.ds(m, CH), :] = side - flat(total)

    def make_images(it, src):
        for m in range(0, N, CH):
            up, mid, down = (
                strips[it, src, p + n, pl.ds(m, CH), :].astype(F32) for n in range(3)
            )
            left = tiled(pltpu.roll(mid, 1, 1))
            right = tiled(pltpu.roll(mid, cols - 1, 1))
            up, mid, down = tiled(up), tiled(mid), tiled(down)
            for f in range(FIELDS):
                value = flat(
                    fco[f, 0] * mid
                    - fco[f, 1] * left
                    - fco[f, 2] * right
                    - fco[f, 3] * up
                    - fco[f, 4] * down
                )
                hi = value.astype(BF16)
                lo = (value - hi.astype(F32)).astype(BF16)
                images[3 * src + f, pl.ds(m, CH), :cols] = hi
                images[3 * src + f, pl.ds(m, CH), cols:] = lo

    for it in range(ITERS):
        last = it == ITERS - 1

        def source_at(k, q):
            return 2 * ((C + D2 - k) % D2) + q

        def relay(k, q):
            src = source_at(k, q)
            shared = strips.at[it, src, 1 + p]
            return remote(shared, shared, ps.at[it, src], pr.at[it, src], partner, s)

        def arrive(k):
            for q in range(2):
                src = source_at(k, q)
                for g in range(2):
                    landed(
                        strips.at[it, src, pl.ds(2 * p, 2), pl.ds(g * HM, HM)], fr.at[it, g, src]
                    )
                relay(k, q).start()

        def imagine(k):
            for q in range(2):
                relay(k, q).wait_recv()
            for q in range(2):
                make_images(it, source_at(k, q))

        @pl.loop(0, D2)
        def _(k):
            apply_mean(2 * k)
            apply_mean(2 * k + 1)

        def load_some(k):
            if it == 0:
                load_coupling(k).start()

        arrive(0)
        load_some(0)
        @pl.loop(1, D2)
        def _(k):
            arrive(k)
            load_some(k)
            imagine(k - 1)

        imagine(D2 - 1)

        if it == 0:

            @pl.loop(0, D2)
            def _(k):
                load_coupling(k).wait()


        def results(i):
            return (
                remote(outq.at[it, i], inq.at[it, d], os_.at[it, 0, i], or_.at[it, 0, d], i, s),
                remote(outs.at[it, i], ins.at[it, d], os_.at[it, 1, i], or_.at[it, 1, d], i, s),
            )

        def mix(i):
            count = count_s[i]
            lefts = []
            rights = []
            for k in range(MAXC):
                entry = jnp.where(k < count, list_s[k, i], 3 * D)
                lefts.append(coup_v[i, k])
                rights.append(images[entry])
            both = jnp.dot(
                jnp.concatenate(lefts, 1),
                jnp.concatenate(rights, 0),
                preferred_element_type=F32,
            )
            value = both[:, :cols] + both[:, cols:]
            peak = jnp.max(jnp.abs(value), axis=0, keepdims=True)
            peak = jnp.maximum(peak, 1e-30)
            outq[it, i] = jnp.round(value * (STEPS / peak)).astype(jnp.int16)
            outs[it, i] = peak * (1.0 / STEPS)

        @pl.loop(1, D2)
        def _(k):
            i = 2 * ((C + k) % D2)
            mix(i)
            mix(i + 1)
            for q in range(2):
                for copy in results(i + q):
                    copy.start()

        mix(2 * C)
        mix(2 * C + 1)
        for copy in results(partner):
            copy.start()
        pltpu.make_async_copy(outq.at[it, d], inq.at[it, d], or_.at[it, 0, d]).start()
        pltpu.make_async_copy(outs.at[it, d], ins.at[it, d], or_.at[it, 1, d]).start()

        if not last:
            low[...] = jnp.zeros((N, cols), F32)

        @pl.loop(0, D2)
        def _(k):
            a = 2 * ((C + 2 * D2 - 1 - k) % D2)
            for q in range(2):
                landed(inq.at[it, a + q], or_.at[it, 0, a + q])
                landed(ins.at[it, a + q], or_.at[it, 1, a + q])
            parts = []
            for q in range(2):
                x = a + q
                plane = r0[x] - inq[it, x].astype(F32) * ins[it, x]
                if last:
                    stage_b[pl.ds(x, N, stride=R), :] = plane
                    rh[x + 1] = transform(plane, fore_v[:, pl.ds(0, 2 * cols)])[0]
                else:
                    rh[x + 1], part = transform(plane, fore_v[...])
                    parts.append(tiled(part) * waves_v[x + 1])
            if not last:
                low[...] += flat(parts[0] + parts[1])

        if last:
            store_r = pltpu.make_async_copy(stage_b, res_h, lsem.at[2])
            store_r.start()

        def swap_low(t):
            mine = low_ex.at[s]
            return remote(mine, mine, zs.at[t], zr.at[s], d, (s + t) % NS)

        if not last:
            low_ex[s] = low[...].astype(BF16)

        def swap(t, g):
            mine = ex.at[it, g, s]
            return remote(mine, mine, xs.at[it, g, t], xr.at[it, g, s], d, (s + t) % NS)

        for g in range(2):

            @pl.loop(0, HM // CH)
            def _(c):
                m = pl.multiple_of(c * CH, CH)
                ms = pl.ds(g * HM + m, CH)
                run = jnp.zeros((CH // 8, 8, cols), F32)
                head = jnp.zeros((CH // 8, 8, cols), F32)
                for x in range(R):
                    value = tiled(rh[x + 1, ms, :])
                    head = head + sweep_v[1, x] * value
                    run = (run + value) * sweep_v[0, x]
                    rh[x + 1, ms, :] = flat(run)
                ex[it, g, s, 0, pl.ds(m, CH), :] = flat(head)
                ex[it, g, s, 1, pl.ds(m, CH), :] = flat(run)

            @pl.loop(1, NS)
            def _(t):
                swap(t, g).start()
                if g == 0 and not last:
                    swap_low(t).start()

        @pl.loop(0, D2)
        def _(k):
            for q in range(2):
                relay(k, q).wait_send()

        sent_pairs(it)

        @pl.loop(1, D)
        def _(t):
            for copy in results((d + t) % D):
                copy.wait_send()

        for g in range(2):

            @pl.loop(1, NS)
            def _(t):
                other = (s + t) % NS
                landed(ex.at[it, g, other], xr.at[it, g, other])

            @pl.loop(0, HM // CH)
            def _(c):
                m = pl.multiple_of(c * CH, CH)
                ms = pl.ds(g * HM + m, CH)
                ends = [tiled(ex[it, g, k % NS, k // NS, pl.ds(m, CH), :]) for k in range(2 * NS)]
                outer = []
                for side_of in range(2):
                    total = meet_v[side_of, 0] * ends[0]
                    for k in range(1, 2 * NS):
                        total = total + meet_v[side_of, k] * ends[k]
                    outer.append(total)
                rh[0, ms, :] = flat(outer[0])
                rh[R + 1, ms, :] = flat(outer[1])
                run = outer[1]
                for x in reversed(range(R)):
                    run = (
                        tiled(rh[x + 1, ms, :]) + sweep_v[2, x] * outer[0] + sweep_v[0, x] * run
                    )
                    rh[x + 1, ms, :] = flat(run)

            half = pl.ds(g * HM, HM)
            if last:

                @pl.loop(0, D2)
                def _(i):
                    for h in range(2):
                        x = 2 * i + h + 1
                        change = transform(rh[x, half, :], back_v[pl.ds(0, 2 * cols), :])[0]
                        whole = pl.ds(g * HM * R + x - 1, HM, stride=R)
                        stage_g[whole, :] = u[x, half, :] + change

                part = pl.ds(g * HM * R, HM * R)
                pltpu.make_async_copy(stage_g.at[part], sol_h.at[part], lsem.at[3 + g]).start()

            else:
                if g == 0:

                    @pl.loop(1, NS)
                    def _(t):
                        other = (s + t) % NS
                        landed(low_ex.at[other], zr.at[other])

                    total = low_ex[0].astype(F32)
                    for k in range(1, NS):
                        total = total + low_ex[k].astype(F32)
                    low[...] = flat(tiled(total) * gap_v[...])

                @pl.loop(0, D2 + 1)
                def _(k):
                    i = (C + k) % (D2 + 1)
                    for h in range(2):
                        x = 2 * i + h
                        wave = flat(tiled(low[half, :]) * waves_v[x]).astype(BF16)
                        plane = u[x, half, :] + transform(rh[x, half, :], back_v[...], wave)[0]
                        u[x, half, :] = plane
                        sb[x, half, :] = plane.astype(BF16)
                    send_pair(it + 1, i, g)

        @pl.loop(1, NS)
        def _(t):
            for g in range(2):
                swap(t, g).wait_send()
            if not last:
                swap_low(t).wait_send()

    store_r.wait()
    for g in range(2):
        part = pl.ds(g * HM * R, HM * R)
        pltpu.make_async_copy(stage_g.at[part], sol_h.at[part], lsem.at[3 + g]).wait()


def local(D, NS, interpret, guess, right_side, mean_coef, field_coef, coupling, listed, count):
    modes, R, cols = guess.shape
    N = BLK
    sine, sweep, meet, waves, gap = tables(R, cols, NS)
    fore = fore_table(sine)
    back = back_table(RELAX * sine.astype(np.float64))
    flat_shape = jax.ShapeDtypeStruct((modes * R, cols), F32)
    hbm = pl.BlockSpec(memory_space=pl.ANY)
    vmem = pl.BlockSpec(memory_space=pltpu.VMEM)
    smem = pl.BlockSpec(memory_space=pltpu.SMEM)
    sems = pltpu.SemaphoreType.DMA
    sol, res = pl.pallas_call(
        functools.partial(body, D, NS, R),
        out_shape=(flat_shape, flat_shape),
        in_specs=[smem, smem, hbm, hbm, vmem, vmem, hbm] + [hbm] * 5 + [vmem],
        out_specs=(hbm, hbm),
        scratch_shapes=[
            pltpu.VMEM((modes * R, cols), F32),
            pltpu.VMEM((modes * R, cols), F32),
            pltpu.VMEM(fore.shape, BF16),
            pltpu.VMEM(back.shape, BF16),
            pltpu.VMEM(sweep.shape, F32),
            pltpu.VMEM(meet.shape[1:], F32),
            pltpu.VMEM(waves.shape[1:], F32),
            pltpu.VMEM((D, MAXC, N, N), BF16),
            pltpu.VMEM((R + 2, N, cols), F32),
            pltpu.VMEM((R + 2, N, cols), BF16),
            pltpu.VMEM((R, N, cols), F32),
            pltpu.VMEM((R + 2, N, cols), F32),
            pltpu.VMEM((ITERS, D, 4, N, cols), BF16),
            pltpu.VMEM((FIELDS * D + 1, N, 2 * cols), BF16),
            pltpu.VMEM((ITERS, D, N, cols), jnp.int16),
            pltpu.VMEM((ITERS, D, 1, cols), F32),
            pltpu.VMEM((ITERS, R, N, cols), jnp.int16),
            pltpu.VMEM((ITERS, R, 1, cols), F32),
            pltpu.VMEM((ITERS, 2, NS, 2, N // 2, cols), F32),
            pltpu.VMEM((N, cols), F32),
            pltpu.VMEM((NS, N, cols), BF16),
            pltpu.VMEM((2, 8, cols), F32),
            pltpu.VMEM((2, 8, cols), F32),
            pltpu.VMEM((FIELDS + 1, R + 16, cols), F32),
            pltpu.VMEM((5, R, 8, cols), F32),
            pltpu.VMEM((FIELDS, 5, 8, cols), F32),
            sems((5,)),
            sems((4,)),
            sems((4,)),
            sems((ITERS, 2, D)),
            sems((ITERS, 2, D)),
            sems((ITERS, D)),
            sems((ITERS, D)),
            sems((ITERS, 2, D)),
            sems((ITERS, 2, D)),
            sems((ITERS, 2, NS)),
            sems((ITERS, 2, NS)),
            sems((NS,)),
            sems((NS,)),
            sems((5,)),
            sems((D // 2,)),
        ],
        compiler_params=pltpu.CompilerParams(
            collective_id=0, has_side_effects=True, vmem_limit_bytes=67043328
        ),
        interpret=interpret,
    )(
        listed.T,
        count,
        guess.reshape(modes * R, cols),
        right_side.reshape(modes * R, cols),
        mean_coef,
        field_coef,
        coupling,
        *(jnp.asarray(table) for table in (fore, back, sweep, meet, waves, gap)),
    )
    return sol.reshape(guess.shape), res.reshape(guess.shape)


def solution(mesh, interpret=False):
    placed = (
        P("mode", "slab", None),
        P("mode", "slab", None),
        P("slab", None),
        P(None, "slab", None),
        P(),
        P(),
        P(),
    )
    return jax.shard_map(
        functools.partial(local, mesh.shape["mode"], mesh.shape["slab"], interpret),
        mesh=mesh,
        in_specs=placed,
        out_specs=(P("mode", "slab", None), P("mode", "slab", None)),
        check_vma=False,
    )
```

```python
import functools
import math

import jax
import jax.numpy as jnp
import numpy as np
from jax import lax
from jax.experimental import pallas as pl
from jax.experimental.pallas import tpu as pltpu
from jax.sharding import PartitionSpec as P

FIELDS = 3
MAXC = 16
BLK = 128
ITERS = 2
RELAX = 0.6
STEPS = 32760.0
F32 = jnp.float32
BF16 = jnp.bfloat16


LOW_ROWS = 8
LOW_COLS = 16


def halves(table):
    hi = np.asarray(table, np.float32).astype(BF16)
    lo = (np.asarray(table, np.float32) - hi.astype(np.float32)).astype(BF16)
    return hi, lo, np.zeros_like(hi)


def fore_table(sine):
    hi, lo, zero = halves(sine)
    low = np.tile(hi[:, :LOW_COLS], (1, LOW_ROWS))
    return np.concatenate(
        [np.concatenate([hi, lo, low], 1), np.concatenate([hi, zero, zero], 1)], 0
    )


def back_table(sine):
    hi, lo, zero = halves(sine)
    low = np.tile(hi[:LOW_COLS], (LOW_ROWS, 1))
    return np.concatenate(
        [
            np.concatenate([hi, lo], 1),
            np.concatenate([hi, zero], 1),
            np.concatenate([low, zero], 1),
        ],
        0,
    )


def single(length):
    f32 = np.float32
    counter = np.arange(length).astype(f32) + f32(1.0)
    angle = f32(math.pi) * counter[:, None] * counter[None] / f32(length + 1)
    sine = np.sin(angle.astype(np.float64)).astype(f32)
    sine = f32(math.sqrt(2.0 / (length + 1))) * sine
    turn = f32(math.pi) * counter / f32(length + 1)
    return sine, f32(2.0) * np.cos(turn.astype(np.float64)).astype(f32)


def tables(rows, cols, slabs):
    length = rows * slabs
    sine, along = single(cols)
    across = single(length)[1]
    diag = 4.0 - along.astype(np.float64)
    pivot = np.zeros((rows, cols))
    pivot[0] = 1.0 / diag
    for x in range(1, rows):
        pivot[x] = 1.0 / (diag - pivot[x - 1])
    reach = np.cumprod(pivot, axis=0)
    first = np.zeros((rows, cols))
    meet = np.zeros((slabs, 2, 2 * slabs, cols))
    eye = np.eye(rows)
    shift = np.eye(rows, k=1) + np.eye(rows, k=-1)
    for q in range(cols):
        column = np.linalg.solve(diag[q] * eye - shift, eye[0])
        first[:, q] = column
        near, far = column[0], column[-1]
        system = np.eye(2 * slabs)
        for s in range(slabs):
            if s > 0:
                system[s, slabs + s - 1] -= near
                system[slabs + s, slabs + s - 1] -= far
            if s < slabs - 1:
                system[s, s + 1] -= far
                system[slabs + s, s + 1] -= near
        inverse = np.linalg.inv(system)
        for s in range(slabs):
            if s > 0:
                meet[s, 0, :, q] = inverse[slabs + s - 1]
            if s < slabs - 1:
                meet[s, 1, :, q] = inverse[s + 1]
    p = np.arange(LOW_ROWS)
    rounded = (np.float32(4.0) - across[:LOW_ROWS, None]) - along[None, :LOW_COLS]
    smooth = diag[None, :LOW_COLS] - 2.0 * np.cos(np.pi * (p + 1.0) / (length + 1))[:, None]
    gap = 1.0 / rounded.astype(np.float64) - 1.0 / smooth
    gap = np.broadcast_to(gap.reshape(1, cols), (8, cols)).astype(np.float32)
    place = np.arange(slabs)[:, None] * rows + np.arange(rows + 2)[None]
    waves = np.sqrt(2.0 / (length + 1)) * np.sin(
        np.pi * place[:, :, None] * (p + 1.0) / (length + 1)
    )
    waves = np.repeat(waves, LOW_COLS, axis=2)
    waves = np.broadcast_to(waves[:, :, None], (slabs, rows + 2, 8, cols)).astype(np.float32)
    sweep = np.stack([pivot, first, reach])
    sweep = np.broadcast_to(sweep[:, :, None], (3, rows, 8, cols)).astype(np.float32)
    meet = np.broadcast_to(meet[:, :, :, None], (slabs, 2, 2 * slabs, 8, cols)).astype(np.float32)
    return sine, sweep, meet, waves, gap


def tiled(plane):
    return plane.reshape(plane.shape[0] // 8, 8, plane.shape[1])


def flat(plane):
    return plane.reshape(plane.shape[0] * 8, plane.shape[2])


def transform(plane, table, extra=None):
    hi = plane.astype(BF16)
    lo = (plane - hi.astype(F32)).astype(BF16)
    parts = [hi, lo] if extra is None else [hi, lo, extra]
    both = jnp.dot(jnp.concatenate(parts, 1), table, preferred_element_type=F32)
    cols = plane.shape[1]
    return both[:, :cols] + both[:, cols : 2 * cols], both[:, 2 * cols :]


def averages(center, above, below):
    cols = center.shape[1]
    lane = lax.broadcasted_iota(jnp.int32, center.shape, 1)
    left = 0.5 * (center + pltpu.roll(center, 1, 1))
    right = 0.5 * (center + pltpu.roll(center, cols - 1, 1))
    up = 0.5 * (center + above)
    down = 0.5 * (center + below)
    zero = jnp.zeros_like(center)
    total = (
        up + down + jnp.where(lane == 0, center, left) + jnp.where(lane == cols - 1, center, right)
    )
    return (
        total,
        jnp.where(lane == 0, zero, left),
        jnp.where(lane == cols - 1, zero, right),
        up,
        down,
    )


def body(
    D,
    NS,
    R,
    list_s,
    count_s,
    guess_h,
    right_h,
    mean_v,
    field_v,
    coup_h,
    fore_h,
    back_h,
    sweep_h,
    meet_h,
    waves_h,
    gap_v,
    sol_h,
    res_h,
    stage_g,
    stage_b,
    fore_v,
    back_v,
    sweep_v,
    meet_v,
    waves_v,
    coup_v,
    u,
    sb,
    r0,
    rh,
    strips,
    images,
    outq,
    outs,
    inq,
    ins,
    ex,
    low,
    low_ex,
    edge,
    edge_in,
    cpad,
    mco,
    fco,
    lsem,
    hs,
    hr,
    fs,
    fr,
    ps,
    pr,
    os_,
    or_,
    xs,
    xr,
    zs,
    zr,
    table_sem,
    coup_sem,
):
    D2 = D // 2
    N = BLK
    cols = guess_h.shape[1]
    d = lax.axis_index("mode")
    s = lax.axis_index("slab")
    C = d // 2
    p = d % 2
    partner = 2 * C + 1 - p
    above = (s + NS - 1) % NS
    below = (s + 1) % NS
    CH = 32

    def remote(src, dst, send, recv, mode, slab):
        return pltpu.make_async_remote_copy(
            src_ref=src,
            dst_ref=dst,
            send_sem=send,
            recv_sem=recv,
            device_id=(mode, slab),
            device_id_type=pl.DeviceIdType.MESH,
        )

    def landed(ref, sem):
        pltpu.make_async_copy(ref, ref, sem).wait()

    HM = N // 2
    load_g = pltpu.make_async_copy(guess_h, stage_g, lsem.at[0])
    load_b = pltpu.make_async_copy(right_h, stage_b, lsem.at[1])
    load_g.start()

    def load_coupling(k):
        some = pl.ds(2 * k, 2)
        return pltpu.make_async_copy(coup_h.at[some], coup_v.at[some], coup_sem.at[k])

    table_loads = [
        pltpu.make_async_copy(source, target, table_sem.at[n])
        for n, (source, target) in enumerate(
            (
                (fore_h, fore_v),
                (back_h, back_v),
                (sweep_h, sweep_v),
                (meet_h.at[s], meet_v),
                (waves_h.at[s], waves_v),
            )
        )
    ]

    barrier = pltpu.get_barrier_semaphore()

    @pl.loop(1, D)
    def _(t):
        pl.semaphore_signal(
            barrier, inc=1, device_id=((d + t) % D, s), device_id_type=pl.DeviceIdType.MESH
        )

    @pl.loop(1, NS)
    def _(t):
        pl.semaphore_signal(
            barrier, inc=1, device_id=(d, (s + t) % NS), device_id_type=pl.DeviceIdType.MESH
        )

    for f in range(FIELDS + 1):
        whole = mean_v[...] if f == 0 else field_v[f - 1]
        cpad[f, pl.ds(8, R), :] = whole
        edge[0, pl.ds(f, 1), :] = whole[:1]
        edge[1, pl.ds(f, 1), :] = whole[R - 1 :]
    images[3 * D] = jnp.zeros((N, 2 * cols), BF16)
    load_g.wait()

    def take(x):
        plane = stage_g[pl.ds(x, N, stride=R), :]
        u[x + 1] = plane
        sb[x + 1] = plane.astype(BF16)

    @pl.loop(0, D2)
    def _(k):
        take(2 * k)
        take(2 * k + 1)

    pl.semaphore_wait(barrier, D - 1 + NS - 1)

    halo_up = remote(u.at[1], u.at[R + 1], hs.at[0], hr.at[0], d, above)
    halo_down = remote(u.at[R], u.at[0], hs.at[1], hr.at[1], d, below)
    coef_up = remote(edge.at[0], edge_in.at[1], hs.at[2], hr.at[2], d, above)
    coef_down = remote(edge.at[1], edge_in.at[0], hs.at[3], hr.at[3], d, below)
    halo_up.start()
    halo_down.start()
    coef_up.start()
    coef_down.start()

    def modes_of(it, g):
        return pl.ds(g * HM, HM) if it else pl.ds(0, N)

    def groups(it):
        return range(2) if it else range(1)

    def pair_copies(it, i, g):
        source = sb.at[pl.ds(2 * i, 2), modes_of(it, g)]
        for live, j, half in ((i < D2, 2 * i, 0), (i >= 1, 2 * i - 1, 1)):
            target = strips.at[it, d, pl.ds(2 * half, 2), modes_of(it, g)]
            yield live, j, source, target

    def send_pair(it, i, g):
        for live, j, source, target in pair_copies(it, i, g):

            @pl.when(jnp.logical_and(live, j != d))
            def _():
                remote(source, target, fs.at[it, g, j], fr.at[it, g, d], j, s).start()

            @pl.when(jnp.logical_and(live, j == d))
            def _():
                pltpu.make_async_copy(source, target, fr.at[it, g, d]).start()

    def sent_pairs(it):
        @pl.loop(1, D)
        def _(t):
            j = (d + t) % D
            for g in groups(it):
                source = sb.at[pl.ds(0, 2), modes_of(it, g)]
                target = strips.at[it, d, pl.ds(0, 2), modes_of(it, g)]
                remote(source, target, fs.at[it, g, j], fr.at[it, g, d], j, s).wait_send()

    @pl.loop(0, D2 - 1)
    def _(k):
        send_pair(0, 1 + (C + D2 - 2 + k) % (D2 - 1), 0)

    load_b.start()
    for copy in table_loads:
        copy.start()

    coef_up.wait()
    coef_down.wait()
    for f in range(FIELDS + 1):
        whole = cpad[f, pl.ds(8, R), :]
        cpad[f, pl.ds(7, 1), :] = jnp.where(s == 0, whole[:1], edge_in[0, pl.ds(f, 1), :])
        cpad[f, pl.ds(8 + R, 1), :] = jnp.where(
            s == NS - 1, whole[R - 1 :], edge_in[1, pl.ds(f, 1), :]
        )
    halo_up.wait()
    halo_down.wait()
    top = jnp.where(s == 0, jnp.zeros((N, cols), F32), u[0])
    bottom = jnp.where(s == NS - 1, jnp.zeros((N, cols), F32), u[R + 1])
    u[0] = top
    u[R + 1] = bottom
    sb[0] = top.astype(BF16)
    sb[R + 1] = bottom.astype(BF16)
    send_pair(0, 0, 0)
    send_pair(0, D2, 0)

    for n, value in enumerate(
        averages(cpad[0, pl.ds(8, R), :], cpad[0, pl.ds(7, R), :], cpad[0, pl.ds(9, R), :])
    ):
        mco[n] = jnp.broadcast_to(value[:, None, :], (R, 8, cols))
    for f in range(FIELDS):
        rows3 = [
            jnp.broadcast_to(cpad[f + 1, pl.ds(7 + d + n, 1), :], (8, cols)) for n in range(3)
        ]
        for n, value in enumerate(averages(rows3[1], rows3[0], rows3[2])):
            fco[f, n] = value
    load_b.wait()
    for copy in table_loads:
        copy.wait()

    def apply_mean(x):
        co = [mco[n, x] for n in range(5)]
        for m in range(0, N, CH):
            mid = u[x + 1, pl.ds(m, CH), :]
            left = pltpu.roll(mid, 1, 1)
            right = pltpu.roll(mid, cols - 1, 1)
            total = co[0] * tiled(mid) - co[1] * tiled(left) - co[2] * tiled(right)
            total = total - co[3] * tiled(u[x, pl.ds(m, CH), :])
            total = total - co[4] * tiled(u[x + 2, pl.ds(m, CH), :])
            side = stage_b[pl.ds(m * R + x, CH, stride=R), :]
            r0[x, pl.ds(m, CH), :] = side - flat(total)

    def make_images(it, src):
        for m in range(0, N, CH):
            up, mid, down = (
                strips[it, src, p + n, pl.ds(m, CH), :].astype(F32) for n in range(3)
            )
            left = tiled(pltpu.roll(mid, 1, 1))
            right = tiled(pltpu.roll(mid, cols - 1, 1))
            up, mid, down = tiled(up), tiled(mid), tiled(down)
            for f in range(FIELDS):
                value = flat(
                    fco[f, 0] * mid
                    - fco[f, 1] * left
                    - fco[f, 2] * right
                    - fco[f, 3] * up
                    - fco[f, 4] * down
                )
                hi = value.astype(BF16)
                lo = (value - hi.astype(F32)).astype(BF16)
                images[3 * src + f, pl.ds(m, CH), :cols] = hi
                images[3 * src + f, pl.ds(m, CH), cols:] = lo

    for it in range(ITERS):
        last = it == ITERS - 1

        def source_at(k, q):
            return 2 * ((C + D2 - k) % D2) + q

        def relay(k, q):
            src = source_at(k, q)
            shared = strips.at[it, src, 1 + p]
            return remote(shared, shared, ps.at[it, src], pr.at[it, src], partner, s)

        def arrive(k):
            for q in range(2):
                src = source_at(k, q)
                for g in groups(it):
                    landed(strips.at[it, src, pl.ds(2 * p, 2), modes_of(it, g)], fr.at[it, g, src])
                relay(k, q).start()

        def imagine(k):
            for q in range(2):
                relay(k, q).wait_recv()
            for q in range(2):
                make_images(it, source_at(k, q))

        @pl.loop(0, D2)
        def _(k):
            apply_mean(2 * k)
            apply_mean(2 * k + 1)

        def load_some(k):
            if it == 0:
                load_coupling(k).start()

        arrive(0)
        load_some(0)
        @pl.loop(1, D2)
        def _(k):
            arrive(k)
            load_some(k)
            imagine(k - 1)

        imagine(D2 - 1)

        if it == 0:

            @pl.loop(0, D2)
            def _(k):
                load_coupling(k).wait()


        def results(i):
            return (
                remote(outq.at[it, i], inq.at[it, d], os_.at[it, 0, i], or_.at[it, 0, d], i, s),
                remote(outs.at[it, i], ins.at[it, d], os_.at[it, 1, i], or_.at[it, 1, d], i, s),
            )

        def mix(i):
            count = count_s[i]
            lefts = []
            rights = []
            for k in range(MAXC):
                entry = jnp.where(k < count, list_s[k, i], 3 * D)
                lefts.append(coup_v[i, k])
                rights.append(images[entry])
            both = jnp.dot(
                jnp.concatenate(lefts, 1),
                jnp.concatenate(rights, 0),
                preferred_element_type=F32,
            )
            value = both[:, :cols] + both[:, cols:]
            peak = jnp.max(jnp.abs(value), axis=0, keepdims=True)
            peak = jnp.maximum(peak, 1e-30)
            outq[it, i] = jnp.round(value * (STEPS / peak)).astype(jnp.int16)
            outs[it, i] = peak * (1.0 / STEPS)

        @pl.loop(1, D2)
        def _(k):
            i = 2 * ((C + k) % D2)
            mix(i)
            mix(i + 1)
            for q in range(2):
                for copy in results(i + q):
                    copy.start()

        mix(2 * C)
        mix(2 * C + 1)
        for copy in results(partner):
            copy.start()
        pltpu.make_async_copy(outq.at[it, d], inq.at[it, d], or_.at[it, 0, d]).start()
        pltpu.make_async_copy(outs.at[it, d], ins.at[it, d], or_.at[it, 1, d]).start()

        if not last:
            low[...] = jnp.zeros((N, cols), F32)

        @pl.loop(0, D2)
        def _(k):
            a = 2 * ((C + 2 * D2 - 1 - k) % D2)
            for q in range(2):
                landed(inq.at[it, a + q], or_.at[it, 0, a + q])
                landed(ins.at[it, a + q], or_.at[it, 1, a + q])
            parts = []
            for q in range(2):
                x = a + q
                plane = r0[x] - inq[it, x].astype(F32) * ins[it, x]
                if last:
                    stage_b[pl.ds(x, N, stride=R), :] = plane
                    rh[x + 1] = transform(plane, fore_v[:, pl.ds(0, 2 * cols)])[0]
                else:
                    rh[x + 1], part = transform(plane, fore_v[...])
                    parts.append(tiled(part) * waves_v[x + 1])
            if not last:
                low[...] += flat(parts[0] + parts[1])

        if last:
            store_r = pltpu.make_async_copy(stage_b, res_h, lsem.at[2])
            store_r.start()

        def swap_low(t):
            mine = low_ex.at[s]
            return remote(mine, mine, zs.at[t], zr.at[s], d, (s + t) % NS)

        if not last:
            low_ex[s] = low[...].astype(BF16)

        def swap(t, g):
            mine = ex.at[it, g, s]
            return remote(mine, mine, xs.at[it, g, t], xr.at[it, g, s], d, (s + t) % NS)

        for g in range(2):

            @pl.loop(0, HM // CH)
            def _(c):
                m = pl.multiple_of(c * CH, CH)
                ms = pl.ds(g * HM + m, CH)
                run = jnp.zeros((CH // 8, 8, cols), F32)
                head = jnp.zeros((CH // 8, 8, cols), F32)
                for x in range(R):
                    value = tiled(rh[x + 1, ms, :])
                    head = head + sweep_v[1, x] * value
                    run = (run + value) * sweep_v[0, x]
                    rh[x + 1, ms, :] = flat(run)
                ex[it, g, s, 0, pl.ds(m, CH), :] = flat(head)
                ex[it, g, s, 1, pl.ds(m, CH), :] = flat(run)

            @pl.loop(1, NS)
            def _(t):
                swap(t, g).start()
                if g == 0 and not last:
                    swap_low(t).start()

        @pl.loop(0, D2)
        def _(k):
            for q in range(2):
                relay(k, q).wait_send()

        sent_pairs(it)

        @pl.loop(1, D)
        def _(t):
            for copy in results((d + t) % D):
                copy.wait_send()

        for g in range(2):

            @pl.loop(1, NS)
            def _(t):
                other = (s + t) % NS
                landed(ex.at[it, g, other], xr.at[it, g, other])

            @pl.loop(0, HM // CH)
            def _(c):
                m = pl.multiple_of(c * CH, CH)
                ms = pl.ds(g * HM + m, CH)
                ends = [tiled(ex[it, g, k % NS, k // NS, pl.ds(m, CH), :]) for k in range(2 * NS)]
                outer = []
                for side_of in range(2):
                    total = meet_v[side_of, 0] * ends[0]
                    for k in range(1, 2 * NS):
                        total = total + meet_v[side_of, k] * ends[k]
                    outer.append(total)
                rh[0, ms, :] = flat(outer[0])
                rh[R + 1, ms, :] = flat(outer[1])
                run = outer[1]
                for x in reversed(range(R)):
                    run = (
                        tiled(rh[x + 1, ms, :]) + sweep_v[2, x] * outer[0] + sweep_v[0, x] * run
                    )
                    rh[x + 1, ms, :] = flat(run)

            half = pl.ds(g * HM, HM)
            if last:

                @pl.loop(0, D2)
                def _(i):
                    for h in range(2):
                        x = 2 * i + h + 1
                        change = transform(rh[x, half, :], back_v[pl.ds(0, 2 * cols), :])[0]
                        whole = pl.ds(g * HM * R + x - 1, HM, stride=R)
                        stage_g[whole, :] = u[x, half, :] + change

                part = pl.ds(g * HM * R, HM * R)
                pltpu.make_async_copy(stage_g.at[part], sol_h.at[part], lsem.at[3 + g]).start()

            else:
                if g == 0:

                    @pl.loop(1, NS)
                    def _(t):
                        other = (s + t) % NS
                        landed(low_ex.at[other], zr.at[other])

                    total = low_ex[0].astype(F32)
                    for k in range(1, NS):
                        total = total + low_ex[k].astype(F32)
                    low[...] = flat(tiled(total) * gap_v[...])

                @pl.loop(0, D2 + 1)
                def _(k):
                    i = (C + k) % (D2 + 1)
                    for h in range(2):
                        x = 2 * i + h
                        wave = flat(tiled(low[half, :]) * waves_v[x]).astype(BF16)
                        plane = u[x, half, :] + transform(rh[x, half, :], back_v[...], wave)[0]
                        u[x, half, :] = plane
                        sb[x, half, :] = plane.astype(BF16)
                    send_pair(it + 1, i, g)

        @pl.loop(1, NS)
        def _(t):
            for g in range(2):
                swap(t, g).wait_send()
            if not last:
                swap_low(t).wait_send()

    store_r.wait()
    for g in range(2):
        part = pl.ds(g * HM * R, HM * R)
        pltpu.make_async_copy(stage_g.at[part], sol_h.at[part], lsem.at[3 + g]).wait()


def local(D, NS, interpret, guess, right_side, mean_coef, field_coef, coupling, listed, count):
    modes, R, cols = guess.shape
    N = BLK
    sine, sweep, meet, waves, gap = tables(R, cols, NS)
    fore = fore_table(sine)
    back = back_table(RELAX * sine.astype(np.float64))
    flat_shape = jax.ShapeDtypeStruct((modes * R, cols), F32)
    hbm = pl.BlockSpec(memory_space=pl.ANY)
    vmem = pl.BlockSpec(memory_space=pltpu.VMEM)
    smem = pl.BlockSpec(memory_space=pltpu.SMEM)
    sems = pltpu.SemaphoreType.DMA
    sol, res = pl.pallas_call(
        functools.partial(body, D, NS, R),
        out_shape=(flat_shape, flat_shape),
        in_specs=[smem, smem, hbm, hbm, vmem, vmem, hbm] + [hbm] * 5 + [vmem],
        out_specs=(hbm, hbm),
        scratch_shapes=[
            pltpu.VMEM((modes * R, cols), F32),
            pltpu.VMEM((modes * R, cols), F32),
            pltpu.VMEM(fore.shape, BF16),
            pltpu.VMEM(back.shape, BF16),
            pltpu.VMEM(sweep.shape, F32),
            pltpu.VMEM(meet.shape[1:], F32),
            pltpu.VMEM(waves.shape[1:], F32),
            pltpu.VMEM((D, MAXC, N, N), BF16),
            pltpu.VMEM((R + 2, N, cols), F32),
            pltpu.VMEM((R + 2, N, cols), BF16),
            pltpu.VMEM((R, N, cols), F32),
            pltpu.VMEM((R + 2, N, cols), F32),
            pltpu.VMEM((ITERS, D, 4, N, cols), BF16),
            pltpu.VMEM((FIELDS * D + 1, N, 2 * cols), BF16),
            pltpu.VMEM((ITERS, D, N, cols), jnp.int16),
            pltpu.VMEM((ITERS, D, 1, cols), F32),
            pltpu.VMEM((ITERS, R, N, cols), jnp.int16),
            pltpu.VMEM((ITERS, R, 1, cols), F32),
            pltpu.VMEM((ITERS, 2, NS, 2, N // 2, cols), F32),
            pltpu.VMEM((N, cols), F32),
            pltpu.VMEM((NS, N, cols), BF16),
            pltpu.VMEM((2, 8, cols), F32),
            pltpu.VMEM((2, 8, cols), F32),
            pltpu.VMEM((FIELDS + 1, R + 16, cols), F32),
            pltpu.VMEM((5, R, 8, cols), F32),
            pltpu.VMEM((FIELDS, 5, 8, cols), F32),
            sems((5,)),
            sems((4,)),
            sems((4,)),
            sems((ITERS, 2, D)),
            sems((ITERS, 2, D)),
            sems((ITERS, D)),
            sems((ITERS, D)),
            sems((ITERS, 2, D)),
            sems((ITERS, 2, D)),
            sems((ITERS, 2, NS)),
            sems((ITERS, 2, NS)),
            sems((NS,)),
            sems((NS,)),
            sems((5,)),
            sems((D // 2,)),
        ],
        compiler_params=pltpu.CompilerParams(
            collective_id=0, has_side_effects=True, vmem_limit_bytes=67043328
        ),
        interpret=interpret,
    )(
        listed.T,
        count,
        guess.reshape(modes * R, cols),
        right_side.reshape(modes * R, cols),
        mean_coef,
        field_coef,
        coupling,
        *(jnp.asarray(table) for table in (fore, back, sweep, meet, waves, gap)),
    )
    return sol.reshape(guess.shape), res.reshape(guess.shape)


def solution(mesh, interpret=False):
    placed = (
        P("mode", "slab", None),
        P("mode", "slab", None),
        P("slab", None),
        P(None, "slab", None),
        P(),
        P(),
        P(),
    )
    return jax.shard_map(
        functools.partial(local, mesh.shape["mode"], mesh.shape["slab"], interpret),
        mesh=mesh,
        in_specs=placed,
        out_specs=(P("mode", "slab", None), P("mode", "slab", None)),
        check_vma=False,
    )
```
